128 devices in a mesh: dp: 16 (over x_lo, z, core), tensor: 8 (over y, x_hi).
Axes of the slice: x: 4 (x_hi: 2, x_lo: 2; x = x_hi * 2 + x_lo), y: 4, z: 4, core: 2. Of those that a mesh axis runs over, the one named last changes fastest.
Arguments:
- out_grad: bfloat16 [4096, 4096], P('dp'), may hold values from -8 to 8
- hidden_act: bfloat16 [4096, 15360], P('dp', 'tensor'), may hold values from -6 to 6
- log_ratio: float32 [128], P('dp'), may hold values from -40 to 40
- pair_order: int32 [16, 8], P('dp'), may hold values from 0 to 7, each once within a row
- seq_len: int32 [128], P('dp'), may hold values from 1 to 32, 2560 in all
- master: float32 [4096, 15360], P('dp', 'tensor'), may hold values from -0.046875 to 0.046875
- moment: float32 [4096, 15360], P('dp', 'tensor'), may hold values from -6 to 6
- second: float32 [4096, 15360], P('dp', 'tensor'), may hold values from 0.005 to 0.08
- next_act: bfloat16 [8192, 15360], P('dp', 'tensor'), may hold values from -6 to 6
Outputs:
- new_master: float32 [4096, 15360], P('dp', 'tensor')
- new_moment: float32 [4096, 15360], P('dp', 'tensor')
- new_second: float32 [4096, 15360], P('dp', 'tensor')
- update: float32 [4096, 15360], P('dp', 'tensor')
- next_out: bfloat16 [8192, 4096], P('dp', 'tensor')
The draws below stay inside these ranges and needn't reach their ends.
Inputs may be any that keep to these rules, and one draw needn't show every extreme that they name: Each row of pair_order holds every number below 8 once.
All inputs are finite; a program needn't handle non-finite values. No bound on the sum of `seq_len` on one device may be relied on, other than what follows from the above.
Results may differ from the reference program's by a relative error of at most 0.02.
Values may be sent and summed in bfloat16 or wider, within the bound.
A program may use at most 128 MiB of HBM per device.

```python
import math
import jax
import jax.numpy as jnp
import numpy as np
from jax import lax

D = 4096
FF = 15360
LEN = 32
TOK_DEV = 256
SEQ_DEV = 8
SEQS = 128
TOKENS = 4096
NEXT = 8192
N_DP = 16
N_TENSOR = 8


def with_spikes(array, stream_key, source, target, shards_of, factor):
    def block_of(dim):
        return (jnp.arange(array.shape[dim]) // (array.shape[dim] // shards_of)).reshape((-1,) + (1,) * (array.ndim - 1 - dim))

    one_side = jax.random.permutation(stream_key, shards_of)[block_of(target)]
    other_side = (block_of(target) + shards_of // 2) % shards_of
    return jnp.where((block_of(source) == one_side) | (block_of(source) == other_side), factor * array, array)


def block_levels(rng, shape, split, low, largest):
    factor_of = 1.0
    for dim, blocks in split:
        draws = jax.random.uniform(jax.random.fold_in(jax.random.fold_in(rng, 6), dim), (blocks,), jnp.float32, low / len(split), largest / len(split))
        factor_of = factor_of * jnp.repeat(jnp.exp(draws), shape[dim] // blocks).reshape((-1,) + (1,) * (len(shape) - 1 - dim))
    return factor_of


def split_up(amount, total, reach, skew):
    loads = [(1 << 20) // math.isqrt(standing ** skew) + 1 for standing in range(2, amount + 1)]
    rest, counts = total - reach - (amount - 1), [1] * (amount - 1)
    while rest > 0:
        candidates = [i for i in range(amount - 1) if counts[i] < reach]
        mass, remaining = sum([loads[i] for i in candidates]), rest
        for i in candidates:
            addition = min(reach - counts[i], max(1, remaining * loads[i] // mass), rest)
            counts[i] = counts[i] + addition
            rest = rest - addition
    return np.array([reach] + counts)


def ragged_sizes(rng, count, total, bound, slope):
    if count == 2:
        one = jax.random.randint(rng, (), max(1, total - bound), min(bound, total - 1) + 1)
        return jnp.stack([one, total - one])
    sizes = jnp.asarray(split_up(count, total, bound, slope), jnp.int32)
    twos = (count - 1) // 2
    donor, sink = sizes[1:1 + 2 * twos:2], sizes[2:2 + 2 * twos:2]
    slack = jnp.minimum(donor - 1, bound - sink)
    moved = jax.random.randint(jax.random.fold_in(rng, 1), (twos,), 0, 1 << 20) % (slack + 1)
    sizes = sizes.at[1:1 + 2 * twos:2].set(donor - moved).at[2:2 + 2 * twos:2].set(sink + moved)
    return sizes[jax.random.permutation(jax.random.fold_in(rng, 2), count)]


def scatter_about(rng, extent, deviation, bound, cuts=(), kind=jnp.bfloat16):
    drawn = jax.random.normal(rng, extent, jnp.float32) * deviation
    if len(cuts) > 0:
        drawn = block_levels(rng, extent, cuts, -0.22, 0.18) * drawn
    return jnp.clip(drawn, min=-bound, max=bound).astype(kind)


def noise_with(rng, shape, deviation, reach, cuts, heavy, kind=jnp.bfloat16):
    entries = deviation * jax.random.normal(rng, shape, jnp.float32)
    if cuts:
        entries = entries * block_levels(rng, shape, cuts, -0.22, 0.18)
    return jnp.clip(with_spikes(entries, jax.random.fold_in(rng, 3), *heavy), -reach, reach).astype(kind)


def setup_inputs(seed: int = 0) -> dict:
    streams_of = jax.random.split(jax.random.key(seed), 10)
    out_grad = noise_with(streams_of[0], (TOKENS, D), 1.0, 8.0, ((0, 16),), (0, 1, 16, 2.0))
    hidden_act = scatter_about(streams_of[1], (TOKENS, FF), 1.0, 6.0, ((0, 16), (1, 8)))
    log_ratio = scatter_about(streams_of[2], (SEQS,), 10.0, 40.0, ((0, 16),), jnp.float32)
    pair_order = jax.vmap(lambda own: jax.random.permutation(own, SEQ_DEV))(jax.random.split(streams_of[3], N_DP)).reshape((N_DP, SEQ_DEV)).astype(jnp.int32)
    seq_len = ragged_sizes(streams_of[4], SEQS, 20 * SEQS, LEN, 0).astype(jnp.int32)
    master = scatter_about(streams_of[5], (D, FF), FF ** -0.5, 0.046875, ((0, 16), (1, 8)), jnp.float32)
    moment = scatter_about(streams_of[6], (D, FF), 1.0, 6.0, ((0, 16), (1, 8)), jnp.float32)
    second = jnp.clip(jnp.exp(math.log(0.08) - 2.7725887 * jax.random.uniform(streams_of[7], (D, FF), jnp.float32) ** block_levels(streams_of[7], (D, FF), ((0, 16), (1, 8)), -0.2, 0.2)), 0.005, 0.08)
    next_act = scatter_about(streams_of[8], (NEXT, FF), 1.0, 6.0, ((0, 16), (1, 8)))
    return dict(out_grad=out_grad, hidden_act=hidden_act, log_ratio=log_ratio, pair_order=pair_order, seq_len=seq_len, master=master, moment=moment, second=second, next_act=next_act)


beta_dpo = 0.1
beta_one = 0.9
beta_two = 0.999
bias_one = 1.0 - 0.9 ** 10
bias_two = 1.0 - 0.999 ** 10
adam_eps = 1e-08
rate_learn = 0.001

def row_factors(ratios, pair_row, lengths):
    seq_count = ratios.shape[0]
    seq_slots = jnp.arange(seq_count, dtype=jnp.int32)
    chosen = pair_row[0::2]
    rejected = pair_row[1::2]
    pick_chosen = (chosen[:, None] == seq_slots[None, :]).astype(jnp.float32)
    pick_rejected = (rejected[:, None] == seq_slots[None, :]).astype(jnp.float32)
    margin = beta_dpo * (lax.optimization_barrier(jnp.sum(pick_chosen * ratios[None, :], axis=1)) - lax.optimization_barrier(jnp.sum(pick_rejected * ratios[None, :], axis=1)))
    weight = beta_dpo * jax.nn.sigmoid(-margin)
    coefficient = lax.optimization_barrier(jnp.sum(weight[:, None] * (pick_rejected - pick_chosen), axis=0))
    position = jnp.arange(LEN, dtype=jnp.int32)
    in_length = (position[None, :] < lengths[:, None]).astype(jnp.float32)
    return coefficient[:, None] * in_length

def adam_step(grad, master, moment, second):
    new_moment = beta_one * moment + (1.0 - beta_one) * grad
    new_second = beta_two * second + (1.0 - beta_two) * grad * grad
    update = new_moment / bias_one / (jnp.sqrt(new_second / bias_two) + adam_eps)
    new_master = master - rate_learn * update
    return (new_master, new_moment, new_second, update)

def reference(out_grad, hidden_act, log_ratio, pair_order, seq_len, master, moment, second, next_act):
    factors = jax.vmap(row_factors)(log_ratio.reshape(N_DP, SEQ_DEV), pair_order, seq_len.reshape(N_DP, SEQ_DEV))
    scaled = (out_grad.astype(jnp.float32) * factors.reshape(-1)[:, None]).astype(jnp.bfloat16)
    grad = jnp.zeros((D, FF), jnp.float32)
    for shard in range(N_DP):
        rows_grad = scaled[shard * TOK_DEV:(shard + 1) * TOK_DEV]
        rows_act = hidden_act[shard * TOK_DEV:(shard + 1) * TOK_DEV]
        term = jnp.dot(rows_grad.T, rows_act, preferred_element_type=jnp.float32)
        grad = grad + lax.optimization_barrier(term.astype(jnp.bfloat16)).astype(jnp.float32)
    new_master, new_moment, new_second, update = adam_step(grad, master, moment, second)
    weights = new_master.astype(jnp.bfloat16)
    block_width = FF // N_TENSOR
    total_next = jnp.zeros((NEXT, D), jnp.float32)
    for column_block in range(N_TENSOR):
        lower = column_block * block_width
        partial_next = jnp.dot(next_act[:, lower:lower + block_width], weights[:, lower:lower + block_width].T, preferred_element_type=jnp.float32)
        total_next = total_next + lax.optimization_barrier(partial_next.astype(jnp.bfloat16)).astype(jnp.float32)
    next_out = total_next.astype(jnp.bfloat16)
    return (new_master, new_moment, new_second, update, next_out)
```

```python
import jax
import jax.numpy as jnp
from jax import lax
from jax.experimental import pallas as pl
from jax.experimental.pallas import tpu as pltpu
from jax.sharding import PartitionSpec as P

LEN = 32
beta_dpo = 0.1
beta_one = 0.9
beta_two = 0.999
bias_one = 1.0 - 0.9**10
bias_two = 1.0 - 0.999**10
adam_eps = 1e-08
rate_learn = 0.001

MESH = pl.DeviceIdType.MESH
F32 = jnp.float32
BF16 = jnp.bfloat16

FL = 1920
BLK = 256
HALF = 128
CHUNKS = ((0, 768), (768, 768), (1536, 384))
EVENTS = ((0, 0), (0, 1), (1, 0), (3, 0), (1, 1), (3, 1), (2, 0), (2, 1))


def mod4(v):
    return lax.rem(v + 8, 4)


def kernel(
    og_hbm, hid_hbm, ratio_ref, pair_ref, len_ref, mas_hbm, mom_hbm, sec_hbm, nact_hbm,
    mas_out, mom_out, sec_out, upd_out, next_out,
    H, SC, ST, SS, OG, ACC, RSS, RSR, MAS, MOM, SEC, WB, NA, XS, XB, YS, YB, NO,
    loc_sem,
    ha_s, ha_r, sa_s, sa_r, sb_s, sb_r, rs_s, rs_r, na_s, na_r, w_s, w_r, x_s, x_r, y_s, y_r,
):
    dp = lax.axis_index("dp")
    tn = lax.axis_index("tensor")
    xl = dp // 8
    z = lax.rem(dp // 2, 4)
    c = lax.rem(dp, 2)
    y = tn // 2
    xh = lax.rem(tn, 2)

    def dev(xl_=None, z_=None, c_=None, y_=None, xh_=None):
        xl_ = xl if xl_ is None else xl_
        z_ = z if z_ is None else z_
        c_ = c if c_ is None else c_
        y_ = y if y_ is None else y_
        xh_ = xh if xh_ is None else xh_
        return (xl_ * 8 + z_ * 2 + c_, y_ * 2 + xh_)

    right, left, far = mod4(z + 1), mod4(z - 1), mod4(z + 2)
    pc = 1 - c

    barrier = pltpu.get_barrier_semaphore()
    for k in range(1, 16):
        idx = lax.rem(xl * 8 + tn + k, 16)
        pl.semaphore_signal(
            barrier, inc=1,
            device_id=((idx // 8) * 8 + z * 2 + c, lax.rem(idx, 8)), device_id_type=MESH)
    for k in range(1, 8):
        idx = lax.rem(z * 2 + c + k, 8)
        pl.semaphore_signal(
            barrier, inc=1, device_id=(xl * 8 + idx, tn), device_id_type=MESH)

    locals_ = []

    def local(src, dst):
        cp = pltpu.make_async_copy(src, dst, loc_sem.at[len(locals_)])
        cp.start()
        locals_.append(cp)
        return cp

    def aligned(v, m):
        return pl.multiple_of(v * m, m)

    qrows = pl.ds(aligned(y, 64), 64)
    og_cp = local(og_hbm.at[qrows, :], OG)
    own_h = local(hid_hbm, H.at[pl.ds(aligned(z * 2 + c, BLK), BLK), :])
    mas_cp = local(mas_hbm, MAS)
    mom_cp = local(mom_hbm, MOM)
    sec_cp = local(sec_hbm, SEC)
    own_na = local(nact_hbm, NA.at[xl])
    pl.semaphore_wait(barrier, 22)

    sends = []

    def remote(src, dst, ss, rs, to):
        return pltpu.make_async_remote_copy(
            src, dst, ss, rs, device_id=to, device_id_type=MESH)

    def send(src, dst, ss, rs, to):
        cp = remote(src, dst, ss, rs, to)
        cp.start()
        sends.append((None, cp))

    def arrived(dst, ss, rs):
        remote(dst, dst, ss, rs, (dp, tn)).wait_recv()

    def hrow(zz, cc, half=None):
        if half is None:
            return pl.ds(aligned(zz * 2 + cc, BLK), BLK)
        return pl.ds(pl.multiple_of((zz * 2 + cc) * BLK + half * HALF, HALF), HALF)

    def h_own(i):
        cs = pl.ds(CHUNKS[i][0], CHUNKS[i][1])
        src = hid_hbm.at[:, cs]
        dst = H.at[hrow(z, c), cs]
        b = i * 9
        send(src, dst, ha_s.at[b], ha_r.at[b], dev(z_=right))
        send(src, dst, ha_s.at[b + 1], ha_r.at[b + 1], dev(z_=left))
        send(src, dst, ha_s.at[b + 2], ha_r.at[b + 2], dev(c_=pc))

    def h_view(i, zz, cc, half=None):
        return H.at[hrow(zz, cc, half), pl.ds(CHUNKS[i][0], CHUNKS[i][1])]

    def h_forward_near(i):
        b = i * 9
        v = h_view(i, left, c)
        arrived(v, ha_s.at[b], ha_r.at[b])
        v0 = h_view(i, left, c, 0)
        send(v0, v0, ha_s.at[b + 5], ha_r.at[b + 5], dev(z_=right))
        send(v, v, ha_s.at[b + 3], ha_r.at[b + 3], dev(c_=pc))
        v = h_view(i, right, c)
        arrived(v, ha_s.at[b + 1], ha_r.at[b + 1])
        v1 = h_view(i, right, c, 1)
        send(v1, v1, ha_s.at[b + 6], ha_r.at[b + 6], dev(z_=left))
        send(v, v, ha_s.at[b + 4], ha_r.at[b + 4], dev(c_=pc))

    def h_forward_far(i):
        b = i * 9
        for half in (0, 1):
            v = h_view(i, far, c, half)
            arrived(v, ha_s.at[b + 5 + half], ha_r.at[b + 5 + half])
            send(v, v, ha_s.at[b + 7 + half], ha_r.at[b + 7 + half], dev(c_=pc))

    def h_rest(i):
        b = i * 9
        arrived(h_view(i, z, pc), ha_s.at[b + 2], ha_r.at[b + 2])
        arrived(h_view(i, left, pc), ha_s.at[b + 3], ha_r.at[b + 3])
        arrived(h_view(i, right, pc), ha_s.at[b + 4], ha_r.at[b + 4])
        for half in (0, 1):
            arrived(h_view(i, far, pc, half), ha_s.at[b + 7 + half], ha_r.at[b + 7 + half])

    def na_send(p):
        rows = pl.ds(p * HALF, HALF)
        send(nact_hbm.at[rows, :], NA.at[xl, rows, :], na_s.at[p], na_r.at[p], dev(xl_=1 - xl))

    h_own(0)
    na_send(0)
    na_send(1)

    lane = lax.broadcasted_iota(jnp.int32, (1, 8), 1)
    ratios = ratio_ref[...]
    coef = jnp.zeros((1, 8), F32)
    for p in range(4):
        oc = (lane == pair_ref[0, 2 * p]).astype(F32)
        orj = (lane == pair_ref[0, 2 * p + 1]).astype(F32)
        margin = beta_dpo * (
            jnp.sum(oc * ratios, axis=1, keepdims=True)
            - jnp.sum(orj * ratios, axis=1, keepdims=True))
        weight = beta_dpo * jax.nn.sigmoid(-margin)
        coef = coef + weight * (orj - oc)
    row = lax.broadcasted_iota(jnp.int32, (64, 8), 0)
    lane64 = lax.broadcasted_iota(jnp.int32, (64, 8), 1)
    upper = (row >= LEN).astype(jnp.int32)
    sel = (lane64 == 2 * y + upper).astype(F32)
    row_coef = jnp.sum(sel * coef, axis=1, keepdims=True)
    row_len = jnp.sum(sel * len_ref[...].astype(F32), axis=1, keepdims=True)
    pos = (row - LEN * upper)[:, 0:1].astype(F32)
    factor = row_coef * (pos < row_len).astype(F32)
    og_cp.wait()
    for dz in range(4):
        for dc in range(2):
            zz = mod4(z + dz)
            cc = c if dc == 0 else pc
            k = dz * 2 + dc
            for b in range(2):
                cols = pl.ds(pl.multiple_of((b * 8 + zz * 2 + cc) * BLK, BLK), BLK)
                SS[k, :, b * BLK:(b + 1) * BLK] = (OG[:, cols].astype(F32) * factor).astype(BF16)
            dst = SC.at[z * 2 + c, qrows, :]
            if k == 0:
                SC[z * 2 + c, qrows, :] = SS[0]
            else:
                send(SS.at[k], dst, sa_s.at[k], sa_r.at[k], dev(z_=zz, c_=cc))
    h_own(1)
    for dz in range(4):
        for dc in range(2):
            k = dz * 2 + dc
            if k:
                zz = mod4(z - dz)
                cc = c if dc == 0 else pc
                arrived(SC.at[zz * 2 + cc, qrows, :], sa_s.at[k], sa_r.at[k])
    for dy in (1, 3, 2):
        v = SC.at[:, qrows, :]
        send(v, v, sb_s.at[dy], sb_r.at[dy], dev(y_=mod4(y + dy)))

    h_forward_near(0)
    h_own(2)

    for dy in (1, 3, 2):
        yy = mod4(y - dy)
        arrived(SC.at[:, pl.ds(aligned(yy, 64), 64), :], sb_s.at[dy], sb_r.at[dy])

    @pl.loop(0, 8)
    def _(k):
        ST[:, pl.ds(aligned(k, BLK), BLK)] = SC[k].T

    def dot_chunk(i):
        lo, width = CHUNKS[i]
        tile = BLK if width % BLK == 0 else width

        for other in (True, False):
            blk = (1 - xl) if other else xl

            @pl.loop(0, width // tile)
            def _(t):
                cols = pl.ds(pl.multiple_of(lo + t * tile, HALF), tile)
                out = jnp.dot(
                    ST[pl.ds(aligned(blk, BLK), BLK), :], H[:, cols],
                    preferred_element_type=F32)
                if other:
                    RSS[:, cols] = out.astype(BF16)
                else:
                    ACC[:, cols] = out

            if other:
                cs = pl.ds(lo, width)
                send(RSS.at[:, cs], RSR.at[:, cs], rs_s.at[i], rs_r.at[i], dev(xl_=1 - xl))

    def wrow(zz, s, cc):
        return pl.ds(pl.multiple_of(((zz * 2 + s) * 2 + cc) * HALF, HALF), HALF)

    def adam_chunk(i):
        lo, width = CHUNKS[i]
        cs = pl.ds(lo, width)
        arrived(RSR.at[:, cs], rs_s.at[i], rs_r.at[i])
        for s in (0, 1):
            wbase = ((z * 2 + s) * 2 + c) * HALF

            @pl.loop(0, HALF // 16)
            def _(r):
                rows = pl.ds(pl.multiple_of(s * HALF + r * 16, 16), 16)
                wrows = pl.ds(pl.multiple_of(wbase + r * 16, 16), 16)
                grad = ACC[rows, cs] + RSR[rows, cs].astype(F32)
                new_moment = beta_one * MOM[rows, cs] + (1.0 - beta_one) * grad
                new_second = beta_two * SEC[rows, cs] + (1.0 - beta_two) * grad * grad
                update = new_moment / bias_one / (jnp.sqrt(new_second / bias_two) + adam_eps)
                new_master = MAS[rows, cs] - rate_learn * update
                MOM[rows, cs] = new_moment
                SEC[rows, cs] = new_second
                ACC[rows, cs] = update
                MAS[rows, cs] = new_master
                WB[wrows, cs] = new_master.astype(BF16)

    own_h.wait()
    h_forward_far(0)
    h_rest(0)
    dot_chunk(0)
    na_send(2)
    h_forward_near(1)
    h_forward_far(1)
    h_rest(1)
    dot_chunk(1)
    na_send(3)
    mas_cp.wait()
    mom_cp.wait()
    sec_cp.wait()
    h_forward_near(2)
    adam_chunk(0)
    h_forward_far(2)
    h_rest(2)
    dot_chunk(2)
    adam_chunk(1)
    adam_chunk(2)

    def w_view(zz, s, cc):
        return WB.at[wrow(zz, s, cc), :]

    for s in (0, 1):
        b = s * 7
        v = w_view(z, s, c)
        send(v, v, w_s.at[b], w_r.at[b], dev(z_=right))
        send(v, v, w_s.at[b + 1], w_r.at[b + 1], dev(z_=left))
        send(v, v, w_s.at[b + 2], w_r.at[b + 2], dev(c_=pc))
    outs = [
        local(MAS, mas_out), local(MOM, mom_out), local(SEC, sec_out), local(ACC, upd_out)]

    def w_wait(zz, s, cc, n):
        arrived(w_view(zz, s, cc), w_s.at[s * 7 + n], w_r.at[s * 7 + n])

    def w_send(zz, s, n, to):
        v = w_view(zz, s, c)
        send(v, v, w_s.at[s * 7 + n], w_r.at[s * 7 + n], to)

    def w_near(s):
        w_wait(left, s, c, 0)
        if s == 0:
            w_send(left, s, 5, dev(z_=right))
        w_send(left, s, 3, dev(c_=pc))
        w_wait(right, s, c, 1)
        if s == 1:
            w_send(right, s, 5, dev(z_=left))
        w_send(right, s, 4, dev(c_=pc))
        w_wait(left, s, pc, 3)
        w_wait(right, s, pc, 4)

    def w_far(s):
        w_wait(far, s, c, 5)
        w_send(far, s, 6, dev(c_=pc))
        w_wait(far, s, pc, 6)

    own_na.wait()

    def na_wait():
        for p in range(4):
            rows = pl.ds(p * HALF, HALF)
            arrived(NA.at[1 - xl, rows, :], na_s.at[p], na_r.at[p])

    conditional = []

    def project(e):
        dz, s = EVENTS[e]
        zz = mod4(z + dz)
        wcols = pl.ds(pl.multiple_of((zz * 2 + s) * BLK, BLK), BLK)
        slot = (dz // 2) * 2 + s
        mine = xl * 2 + xh
        same_xh = lax.rem(zz, 2) == xh

        @pl.loop(0, 4)
        def _(t):
            blk = t // 2
            rows = pl.ds(aligned(lax.rem(t, 2), BLK), BLK)
            out = lax.dot_general(
                NA[blk, rows, :], WB[wcols, :], (((1,), (1,)), ((), ())),
                preferred_element_type=F32)
            XS[e, blk, rows, :] = out.astype(BF16)

        for dx in (0, 1):
            blk = xl if dx == 0 else 1 - xl
            cp = remote(
                XS.at[e, blk], XB.at[slot, mine], x_s.at[e * 2 + dx], x_r.at[slot * 4 + mine],
                dev(xl_=blk, xh_=lax.rem(zz, 2)))
            if dx == 0:
                go = jnp.logical_not(same_xh)

                @pl.when(go)
                def _():
                    cp.start()

                @pl.when(same_xh)
                def _():
                    XB[slot, mine] = XS[e, blk]

                conditional.append((go, cp))
            else:
                cp.start()
                conditional.append((None, cp))

    def pair_sum(e):
        dz, s = EVENTS[e]
        zz = mod4(z + dz)
        slot = (dz // 2) * 2 + s
        for_me = lax.rem(zz, 2) == xh
        for h in (0, 1):
            yd = zz // 2 + 2 * h
            k = slot * 2 + h

            @pl.when(for_me)
            def _():
                for g in (0, 1):
                    src = h * 2 + g

                    @pl.when(src != xl * 2 + xh)
                    def _():
                        arrived(XB.at[slot, src], x_s.at[0], x_r.at[slot * 4 + src])

                @pl.loop(0, 4)
                def _(r):
                    rows = pl.ds(aligned(r, HALF), HALF)
                    YS[k, rows, :] = (
                        XB[slot, h * 2, rows, :].astype(F32)
                        + XB[slot, h * 2 + 1, rows, :].astype(F32)).astype(BF16)

            cp = remote(
                YS.at[k], YB.at[s, y], y_s.at[k], y_r.at[s * 4 + y], dev(y_=yd))
            go = jnp.logical_and(for_me, yd != y)
            stay = jnp.logical_and(for_me, yd == y)

            @pl.when(go)
            def _():
                cp.start()

            @pl.when(stay)
            def _():
                YB[s, y] = YS[k]

            return_later.append((go, cp))

    return_later = []

    w_wait(z, 0, pc, 2)
    na_wait()
    project(0)
    w_wait(z, 1, pc, 2)
    w_near(0)
    project(1)
    project(2)
    project(3)
    w_near(1)
    pair_sum(0)
    pair_sum(1)
    project(4)
    project(5)
    w_far(0)
    w_far(1)
    project(6)
    project(7)
    for e in range(2, 8):
        pair_sum(e)

    for s in (0, 1):
        for ys in range(4):
            @pl.when(ys != y)
            def _():
                arrived(YB.at[s, ys], y_s.at[0], y_r.at[s * 4 + ys])

        @pl.loop(0, 4)
        def _(r):
            rows = pl.ds(aligned(r, HALF), HALF)
            total = (YB[s, 0, rows, :].astype(F32) + YB[s, 1, rows, :].astype(F32)) + (
                YB[s, 2, rows, :].astype(F32) + YB[s, 3, rows, :].astype(F32))
            total = total.astype(BF16)
            NO[rows, s * HALF:(s + 1) * HALF] = total[:, :HALF]
            NO[rows, BLK + s * HALF:BLK + (s + 1) * HALF] = total[:, HALF:]

    outs.append(local(NO, next_out))
    for go, cp in sends + conditional + return_later:
        if go is None:
            cp.wait_send()
        else:
            @pl.when(go)
            def _():
                cp.wait_send()
    for cp in outs:
        cp.wait()


def body(out_grad, hidden_act, log_ratio, pair_order, seq_len, master, moment, second, next_act):
    block = jax.ShapeDtypeStruct((BLK, FL), F32)
    any_ = pl.BlockSpec(memory_space=pl.ANY)
    vm = pl.BlockSpec(memory_space=pltpu.VMEM)
    dma = pltpu.SemaphoreType.DMA
    return tuple(pl.pallas_call(
        kernel,
        name="fused_step",
        out_shape=(block, block, block, block, jax.ShapeDtypeStruct((512, 512), BF16)),
        in_specs=[any_, any_, vm, pl.BlockSpec(memory_space=pltpu.SMEM), vm, any_, any_, any_, any_],
        out_specs=[any_] * 5,
        scratch_shapes=[
            pltpu.VMEM((8 * BLK, FL), BF16),
            pltpu.VMEM((8, BLK, 512), BF16),
            pltpu.VMEM((512, 8 * BLK), BF16),
            pltpu.VMEM((8, 64, 512), BF16),
            pltpu.VMEM((64, 4096), BF16),
            pltpu.VMEM((BLK, FL), F32),
            pltpu.VMEM((BLK, FL), BF16),
            pltpu.VMEM((BLK, FL), BF16),
            pltpu.VMEM((BLK, FL), F32),
            pltpu.VMEM((BLK, FL), F32),
            pltpu.VMEM((BLK, FL), F32),
            pltpu.VMEM((8 * BLK, FL), BF16),
            pltpu.VMEM((2, 512, FL), BF16),
            pltpu.VMEM((8, 2, 512, BLK), BF16),
            pltpu.VMEM((4, 4, 512, BLK), BF16),
            pltpu.VMEM((8, 512, BLK), BF16),
            pltpu.VMEM((2, 4, 512, BLK), BF16),
            pltpu.VMEM((512, 512), BF16),
            dma((16,)),
            dma((27,)), dma((27,)), dma((8,)), dma((8,)), dma((4,)), dma((4,)),
            dma((3,)), dma((3,)), dma((4,)), dma((4,)), dma((14,)), dma((14,)),
            dma((16,)), dma((16,)), dma((8,)), dma((8,)),
        ],
        compiler_params=pltpu.CompilerParams(
            collective_id=0, has_side_effects=True, vmem_limit_bytes=62 << 20),
    )(out_grad, hidden_act, log_ratio.reshape(1, 8), pair_order, seq_len.reshape(1, 8),
      master, moment, second, next_act))


def solution(mesh):
    return jax.shard_map(
        body,
        mesh=mesh,
        in_specs=(
            P("dp", None), P("dp", "tensor"), P("dp"), P("dp", None), P("dp"),
            P("dp", "tensor"), P("dp", "tensor"), P("dp", "tensor"), P("dp", "tensor"),
        ),
        out_specs=(P("dp", "tensor"),) * 5,
        check_vma=False,
    )
```

```python
import jax
import jax.numpy as jnp
from jax import lax
from jax.experimental import pallas as pl
from jax.experimental.pallas import tpu as pltpu
from jax.sharding import PartitionSpec as P

LEN = 32
beta_dpo = 0.1
beta_one = 0.9
beta_two = 0.999
bias_one = 1.0 - 0.9**10
bias_two = 1.0 - 0.999**10
adam_eps = 1e-08
rate_learn = 0.001

MESH = pl.DeviceIdType.MESH
F32 = jnp.float32
BF16 = jnp.bfloat16

FL = 1920
BLK = 256
HALF = 128
CHUNKS = ((0, 384), (384, 512), (896, 512), (1408, 384), (1792, 128))
UNIT = 64


def mod4(v):
    return lax.rem(v + 8, 4)


def kernel(
    og_hbm, hid_hbm, ratio_ref, pair_ref, len_ref, mas_hbm, mom_hbm, sec_hbm, nact_hbm,
    MAS, MOM, SEC, ACC, NO,
    H, SC, ST, SS, OG, RSS, RSR, WB, NA, XS, XB, YS, YB, YF,
    loc_sem,
    ha_s, ha_r, sa_s, sa_r, sb_s, sb_r, rs_s, rs_r, na_s, na_r, w_s, w_r, x_s, x_r, y_s, y_r, f_s, f_r,
):
    dp = lax.axis_index("dp")
    tn = lax.axis_index("tensor")
    xl = dp // 8
    z = lax.rem(dp // 2, 4)
    c = lax.rem(dp, 2)
    y = tn // 2
    xh = lax.rem(tn, 2)

    def dev(xl_=None, z_=None, c_=None, y_=None, xh_=None):
        xl_ = xl if xl_ is None else xl_
        z_ = z if z_ is None else z_
        c_ = c if c_ is None else c_
        y_ = y if y_ is None else y_
        xh_ = xh if xh_ is None else xh_
        return (xl_ * 8 + z_ * 2 + c_, y_ * 2 + xh_)

    right, left, far = mod4(z + 1), mod4(z - 1), mod4(z + 2)
    pc = 1 - c

    barrier = pltpu.get_barrier_semaphore()
    for k in range(1, 16):
        idx = lax.rem(xl * 8 + tn + k, 16)
        pl.semaphore_signal(
            barrier, inc=1,
            device_id=((idx // 8) * 8 + z * 2 + c, lax.rem(idx, 8)), device_id_type=MESH)
    for k in range(1, 8):
        idx = lax.rem(z * 2 + c + k, 8)
        pl.semaphore_signal(
            barrier, inc=1, device_id=(xl * 8 + idx, tn), device_id_type=MESH)

    locals_ = []

    def local(src, dst):
        cp = pltpu.make_async_copy(src, dst, loc_sem.at[len(locals_)])
        cp.start()
        locals_.append(cp)
        return cp

    def aligned(v, m):
        return pl.multiple_of(v * m, m)

    qrows = pl.ds(aligned(y, 64), 64)
    og_cp = local(og_hbm.at[qrows, :], OG)
    own_h = local(hid_hbm, H.at[pl.ds(aligned(z * 2 + c, BLK), BLK), :])
    mas_cp = local(mas_hbm, MAS)
    mom_cp = local(mom_hbm, MOM)
    sec_cp = local(sec_hbm, SEC)
    own_na = local(nact_hbm, NA.at[xl])
    sends = []

    def remote(src, dst, ss, rs, to):
        return pltpu.make_async_remote_copy(
            src, dst, ss, rs, device_id=to, device_id_type=MESH)

    def send(src, dst, ss, rs, to):
        cp = remote(src, dst, ss, rs, to)
        cp.start()
        sends.append((None, cp))

    def arrived(dst, ss, rs):
        remote(dst, dst, ss, rs, (dp, tn)).wait_recv()

    def hrow(zz, cc, half=None):
        if half is None:
            return pl.ds(aligned(zz * 2 + cc, BLK), BLK)
        return pl.ds(pl.multiple_of((zz * 2 + cc) * BLK + half * HALF, HALF), HALF)

    def h_own(i):
        cs = pl.ds(CHUNKS[i][0], CHUNKS[i][1])
        src = hid_hbm.at[:, cs]
        dst = H.at[hrow(z, c), cs]
        b = i * 9
        send(src, dst, ha_s.at[b], ha_r.at[b], dev(z_=right))
        send(src, dst, ha_s.at[b + 1], ha_r.at[b + 1], dev(z_=left))
        send(src, dst, ha_s.at[b + 2], ha_r.at[b + 2], dev(c_=pc))

    def h_view(i, zz, cc, half=None):
        return H.at[hrow(zz, cc, half), pl.ds(CHUNKS[i][0], CHUNKS[i][1])]

    def h_forward_near(i):
        b = i * 9
        v = h_view(i, left, c)
        arrived(v, ha_s.at[b], ha_r.at[b])
        v0 = h_view(i, left, c, 0)
        send(v0, v0, ha_s.at[b + 5], ha_r.at[b + 5], dev(z_=right))
        send(v, v, ha_s.at[b + 3], ha_r.at[b + 3], dev(c_=pc))
        v = h_view(i, right, c)
        arrived(v, ha_s.at[b + 1], ha_r.at[b + 1])
        v1 = h_view(i, right, c, 1)
        send(v1, v1, ha_s.at[b + 6], ha_r.at[b + 6], dev(z_=left))
        send(v, v, ha_s.at[b + 4], ha_r.at[b + 4], dev(c_=pc))

    def h_forward_far(i):
        b = i * 9
        for half in (0, 1):
            v = h_view(i, far, c, half)
            arrived(v, ha_s.at[b + 5 + half], ha_r.at[b + 5 + half])
            send(v, v, ha_s.at[b + 7 + half], ha_r.at[b + 7 + half], dev(c_=pc))

    def h_rest(i):
        b = i * 9
        arrived(h_view(i, z, pc), ha_s.at[b + 2], ha_r.at[b + 2])
        arrived(h_view(i, left, pc), ha_s.at[b + 3], ha_r.at[b + 3])
        arrived(h_view(i, right, pc), ha_s.at[b + 4], ha_r.at[b + 4])
        for half in (0, 1):
            arrived(h_view(i, far, pc, half), ha_s.at[b + 7 + half], ha_r.at[b + 7 + half])

    def na_send(p):
        rows = pl.ds(p * HALF, HALF)
        send(nact_hbm.at[rows, :], NA.at[xl, rows, :], na_s.at[p], na_r.at[p], dev(xl_=1 - xl))

    lane = lax.broadcasted_iota(jnp.int32, (1, 8), 1)
    ratios = ratio_ref[...]
    coef = jnp.zeros((1, 8), F32)
    for p in range(4):
        oc = (lane == pair_ref[0, 2 * p]).astype(F32)
        orj = (lane == pair_ref[0, 2 * p + 1]).astype(F32)
        margin = beta_dpo * (
            jnp.sum(oc * ratios, axis=1, keepdims=True)
            - jnp.sum(orj * ratios, axis=1, keepdims=True))
        weight = beta_dpo * jax.nn.sigmoid(-margin)
        coef = coef + weight * (orj - oc)
    row = lax.broadcasted_iota(jnp.int32, (64, 8), 0)
    lane64 = lax.broadcasted_iota(jnp.int32, (64, 8), 1)
    upper = (row >= LEN).astype(jnp.int32)
    sel = (lane64 == 2 * y + upper).astype(F32)
    row_coef = jnp.sum(sel * coef, axis=1, keepdims=True)
    row_len = jnp.sum(sel * len_ref[...].astype(F32), axis=1, keepdims=True)
    pos = (row - LEN * upper)[:, 0:1].astype(F32)
    factor = row_coef * (pos < row_len).astype(F32)
    og_cp.wait()

    def scale(b):
        xlb = (1 - xl) if b == 0 else xl
        for dz in range(4):
            for dc in range(2):
                zz = mod4(z + dz)
                cc = c if dc == 0 else pc
                k = dz * 2 + dc
                cols = pl.ds(aligned(xlb * 8 + zz * 2 + cc, BLK), BLK)
                rows = (OG[:, cols].astype(F32) * factor).astype(BF16)
                if k == 0:
                    SC[b, z * 2 + c, qrows, :] = rows
                else:
                    SS[b, k] = rows

    def scale_send(b):
        for dz in range(4):
            for dc in range(2):
                zz = mod4(z + dz)
                cc = c if dc == 0 else pc
                k = dz * 2 + dc
                if k:
                    send(SS.at[b, k], SC.at[b, z * 2 + c, qrows, :],
                         sa_s.at[b * 8 + k], sa_r.at[b * 8 + k], dev(z_=zz, c_=cc))

    def share_rows(b):
        for dz in range(4):
            for dc in range(2):
                k = dz * 2 + dc
                if k:
                    zz = mod4(z - dz)
                    cc = c if dc == 0 else pc
                    arrived(SC.at[b, zz * 2 + cc, qrows, :], sa_s.at[b * 8 + k], sa_r.at[b * 8 + k])
        for dy in (1, 3, 2):
            v = SC.at[b, :, qrows, :]
            send(v, v, sb_s.at[b * 4 + dy], sb_r.at[b * 4 + dy], dev(y_=mod4(y + dy)))

    def turn(b):
        for dy in (1, 3, 2):
            yy = mod4(y - dy)
            arrived(SC.at[b, :, pl.ds(aligned(yy, 64), 64), :],
                    sb_s.at[b * 4 + dy], sb_r.at[b * 4 + dy])

        @pl.loop(0, 8)
        def _(k):
            ST[b, :, pl.ds(aligned(k, BLK), BLK)] = SC[b, k].T

    def dot_chunk(i, b):
        cs = pl.ds(CHUNKS[i][0], CHUNKS[i][1])
        out = jnp.dot(ST[b], H[:, cs], preferred_element_type=F32)
        if b == 0:
            RSS[:, cs] = out.astype(BF16)
            send(RSS.at[:, cs], RSR.at[:, cs], rs_s.at[i], rs_r.at[i], dev(xl_=1 - xl))
        else:
            ACC[:, cs] = out

    def adam_chunk(i):
        lo, width = CHUNKS[i]
        cs = pl.ds(lo, width)
        arrived(RSR.at[:, cs], rs_s.at[i], rs_r.at[i])
        for s in (0, 1):
            wbase = ((z * 2 + s) * 2 + c) * HALF

            @pl.loop(0, HALF // 16)
            def _(r):
                rows = pl.ds(pl.multiple_of(s * HALF + r * 16, 16), 16)
                wrows = pl.ds(pl.multiple_of(wbase + r * 16, 16), 16)
                grad = ACC[rows, cs] + RSR[rows, cs].astype(F32)
                new_moment = beta_one * MOM[rows, cs] + (1.0 - beta_one) * grad
                new_second = beta_two * SEC[rows, cs] + (1.0 - beta_two) * grad * grad
                update = new_moment / bias_one / (jnp.sqrt(new_second / bias_two) + adam_eps)
                new_master = MAS[rows, cs] - rate_learn * update
                MOM[rows, cs] = new_moment
                SEC[rows, cs] = new_second
                ACC[rows, cs] = update
                MAS[rows, cs] = new_master
                WB[wrows, cs] = new_master.astype(BF16)

    scale(0)
    scale(1)
    pl.semaphore_wait(barrier, 22)
    scale_send(0)
    h_own(0)
    na_send(0)
    na_send(1)
    scale_send(1)
    h_own(1)
    share_rows(0)
    h_forward_near(0)
    h_own(2)
    share_rows(1)
    h_forward_near(1)
    h_own(3)
    h_forward_far(0)
    own_h.wait()
    turn(0)
    h_rest(0)
    dot_chunk(0, 0)
    h_forward_near(2)
    h_own(4)
    h_forward_far(1)
    h_rest(1)
    dot_chunk(1, 0)
    h_forward_near(3)
    h_forward_far(2)
    h_rest(2)
    dot_chunk(2, 0)
    turn(1)
    dot_chunk(0, 1)
    h_forward_near(4)
    h_forward_far(3)
    h_rest(3)
    dot_chunk(3, 0)
    mas_cp.wait()
    mom_cp.wait()
    sec_cp.wait()
    adam_chunk(0)
    dot_chunk(1, 1)
    adam_chunk(1)
    dot_chunk(2, 1)
    h_forward_far(4)
    h_rest(4)
    dot_chunk(4, 0)
    na_send(2)
    na_send(3)
    adam_chunk(2)
    dot_chunk(3, 1)
    dot_chunk(4, 1)
    adam_chunk(3)
    adam_chunk(4)

    def w_view(zz, u, cc):
        row = ((zz * 2 + u // 2) * 2 + cc) * HALF + (u % 2) * UNIT
        return WB.at[pl.ds(pl.multiple_of(row, UNIT), UNIT), :]

    def w_send(zz, u, n, to):
        v = w_view(zz, u, c)
        send(v, v, w_s.at[u * 7 + n], w_r.at[u * 7 + n], to)

    def w_wait(zz, u, cc, n):
        arrived(w_view(zz, u, cc), w_s.at[u * 7 + n], w_r.at[u * 7 + n])

    def w_own(u):
        w_send(z, u, 0, dev(z_=right))
        w_send(z, u, 1, dev(z_=left))

    def w_near(u):
        w_wait(left, u, c, 0)
        if u % 2 == 0:
            w_send(left, u, 5, dev(z_=right))
        w_send(left, u, 3, dev(c_=pc))
        w_wait(right, u, c, 1)
        if u % 2 == 1:
            w_send(right, u, 5, dev(z_=left))
        w_send(right, u, 4, dev(c_=pc))

    def w_near_rest(u):
        w_wait(left, u, pc, 3)
        w_wait(right, u, pc, 4)

    def w_far(u):
        w_wait(far, u, c, 5)
        w_send(far, u, 6, dev(c_=pc))

    for u in range(4):
        w_send(z, u, 2, dev(c_=pc))
        if u < 3:
            w_own(u)
    own_na.wait()

    def na_wait():
        for p in range(4):
            rows = pl.ds(p * HALF, HALF)
            arrived(NA.at[1 - xl, rows, :], na_s.at[p], na_r.at[p])

    conditional = []

    zzs = (z, 3 - z, mod4(5 - z), far)
    role = mod4(y - 2 * xl)

    def multiply(kind, s, side):
        wcols = pl.ds(aligned(zzs[kind] * 2 + s, BLK), BLK)
        e = kind * 2 + s
        blk = xl if side == 0 else 1 - xl

        @pl.loop(0, 2)
        def _(t):
            rows = pl.ds(aligned(t, BLK), BLK)
            out = lax.dot_general(
                NA[blk, rows, :], WB[wcols, :], (((1,), (1,)), ((), ())),
                preferred_element_type=F32)
            XS[e, side, rows, :] = out.astype(BF16)

    def start_if(go, cp):
        @pl.when(go)
        def _():
            cp.start()

        conditional.append((go, cp))

    def y_start(kind, s, side):
        multiply(kind, s, side)
        e = kind * 2 + s
        n = e * 2 + side
        h = zzs[kind] // 2
        src = XS.at[e, side]
        start_if(role == 2 + h, remote(
            src, YF.at[n, 0], f_s.at[n], f_r.at[2 * n], dev(y_=mod4(2 * xl + 3 - h))))
        start_if(role == 1 - h, remote(
            src, YF.at[n, 1], f_s.at[n], f_r.at[2 * n + 1], dev(y_=2 * xl + h)))

    def y_middle(kind, s, side):
        e = kind * 2 + s
        n = e * 2 + side
        h = zzs[kind] // 2
        go = role == 3 - h

        @pl.when(go)
        def _():
            arrived(YF.at[n, 0], f_s.at[n], f_r.at[2 * n])

            @pl.loop(0, 4)
            def _(r):
                rows = pl.ds(aligned(r, HALF), HALF)
                XS[e, side, rows, :] = (
                    XS[e, side, rows, :].astype(F32) + YF[n, 0, rows, :].astype(F32)).astype(BF16)

        start_if(go, remote(
            XS.at[e, side], YF.at[n, 0], f_s.at[n], f_r.at[2 * n], dev(y_=2 * xl + h)))

    def y_end(kind, s, side):
        e = kind * 2 + s
        n = e * 2 + side
        zz = zzs[kind]
        h = zz // 2
        last = role == h
        blk = xl if side == 0 else 1 - xl

        @pl.when(last)
        def _():
            for g in (0, 1):
                arrived(YF.at[n, g], f_s.at[n], f_r.at[2 * n + g])

            @pl.loop(0, 4)
            def _(r):
                rows = pl.ds(aligned(r, HALF), HALF)
                XS[e, side, rows, :] = (
                    (XS[e, side, rows, :].astype(F32) + YF[n, 1, rows, :].astype(F32))
                    + YF[n, 0, rows, :].astype(F32)).astype(BF16)

        cp = remote(XS.at[e, side], YB.at[s, xh], f_s.at[n], y_r.at[s * 4 + xh],
                    dev(xl_=blk, xh_=lax.rem(zz, 2)))
        if side == 0:
            same = lax.rem(zz, 2) == xh
            start_if(jnp.logical_and(last, jnp.logical_not(same)), cp)

            @pl.when(jnp.logical_and(last, same))
            def _():
                YB[s, xh] = XS[e, side]
        else:
            start_if(last, cp)

    def x_start(kind, s, side):
        multiply(kind, s, side)
        e = kind * 2 + s
        zz = zzs[kind]
        mine = xl * 2 + xh
        blk = xl if side == 0 else 1 - xl
        cp = remote(
            XS.at[e, side], XB.at[s, mine], x_s.at[(e - 4) * 2 + side], x_r.at[s * 4 + mine],
            dev(xl_=blk, xh_=lax.rem(zz, 2)))
        if side == 0:
            stay = lax.rem(zz, 2) == xh
            start_if(jnp.logical_not(stay), cp)

            @pl.when(stay)
            def _():
                XB[s, mine] = XS[e, side]
        else:
            cp.start()
            conditional.append((None, cp))

    def pair_sum(kind, s, side):
        zz = zzs[kind]
        for_me = lax.rem(zz, 2) == xh
        h = xl if side == 0 else 1 - xl
        yd = zz // 2 + 2 * h
        k = s * 2 + side

        @pl.when(for_me)
        def _():
            for g in (0, 1):
                src = h * 2 + g
                if side == 0:
                    @pl.when(g != xh)
                    def _():
                        arrived(XB.at[s, src], x_s.at[0], x_r.at[s * 4 + src])
                else:
                    arrived(XB.at[s, src], x_s.at[0], x_r.at[s * 4 + src])

            @pl.loop(0, 4)
            def _(r):
                rows = pl.ds(aligned(r, HALF), HALF)
                YS[k, rows, :] = (
                    XB[s, h * 2, rows, :].astype(F32)
                    + XB[s, h * 2 + 1, rows, :].astype(F32)).astype(BF16)

        start_if(jnp.logical_and(for_me, yd != y), remote(
            YS.at[k], YB.at[s, y], y_s.at[k], y_r.at[s * 4 + y], dev(y_=yd)))

        @pl.when(jnp.logical_and(for_me, yd == y))
        def _():
            YB[s, y] = YS[k]

    for u in range(4):
        w_wait(z, u, pc, 2)
    y_start(0, 0, 0)
    y_start(0, 1, 0)
    w_near(0)
    w_near(1)
    w_own(3)
    w_near_rest(0)
    w_near_rest(1)
    y_start(1, 0, 0)
    x_start(2, 0, 0)
    y_middle(0, 0, 0)
    y_middle(0, 1, 0)
    w_near(2)
    w_far(0)
    w_far(1)
    na_wait()
    x_start(2, 0, 1)
    y_start(0, 0, 1)
    y_start(0, 1, 1)
    y_start(1, 0, 1)
    w_wait(far, 0, pc, 6)
    w_wait(far, 1, pc, 6)
    x_start(3, 0, 0)
    x_start(3, 0, 1)
    y_middle(1, 0, 0)
    y_end(0, 0, 0)
    y_end(0, 1, 0)
    w_near(3)
    w_near_rest(2)
    w_near_rest(3)
    for side in (0, 1):
        x_start(2, 1, side)
        y_start(1, 1, side)
    y_middle(0, 0, 1)
    y_middle(0, 1, 1)
    y_middle(1, 0, 1)
    pair_sum(2, 0, 0)
    pair_sum(2, 0, 1)
    w_far(2)
    w_far(3)
    w_wait(far, 2, pc, 6)
    w_wait(far, 3, pc, 6)
    x_start(3, 1, 0)
    x_start(3, 1, 1)
    y_end(1, 0, 0)
    y_end(0, 0, 1)
    y_end(0, 1, 1)
    y_end(1, 0, 1)
    y_middle(1, 1, 0)
    y_middle(1, 1, 1)
    pair_sum(3, 0, 0)
    pair_sum(3, 0, 1)
    pair_sum(2, 1, 0)
    pair_sum(2, 1, 1)
    y_end(1, 1, 0)
    y_end(1, 1, 1)
    pair_sum(3, 1, 0)
    pair_sum(3, 1, 1)

    zd = lax.rem(y, 2) * 2 + xh
    by_y = jnp.logical_or(zd == z, zd == 3 - z)
    by_x = jnp.logical_not(by_y)

    def finish(s, count):
        @pl.loop(0, 4)
        def _(r):
            rows = pl.ds(aligned(r, HALF), HALF)
            total = YB[s, 0, rows, :].astype(F32) + YB[s, 1, rows, :].astype(F32)
            if count == 4:
                total = total + (YB[s, 2, rows, :].astype(F32) + YB[s, 3, rows, :].astype(F32))
            total = total.astype(BF16)
            NO[rows, s * HALF:(s + 1) * HALF] = total[:, :HALF]
            NO[rows, BLK + s * HALF:BLK + (s + 1) * HALF] = total[:, HALF:]

    for s in (0, 1):
        for g in (0, 1):
            away = jnp.logical_or(y // 2 != xl, g != xh)

            @pl.when(jnp.logical_and(by_y, away))
            def _():
                arrived(YB.at[s, g], y_s.at[0], y_r.at[s * 4 + g])

        for ys in range(4):
            @pl.when(jnp.logical_and(by_x, ys != y))
            def _():
                arrived(YB.at[s, ys], y_s.at[0], y_r.at[s * 4 + ys])

        @pl.when(by_y)
        def _():
            finish(s, 2)

        @pl.when(by_x)
        def _():
            finish(s, 4)

    for go, cp in sends + conditional:
        if go is None:
            cp.wait_send()
        else:
            @pl.when(go)
            def _():
                cp.wait_send()


def body(out_grad, hidden_act, log_ratio, pair_order, seq_len, master, moment, second, next_act):
    block = jax.ShapeDtypeStruct((BLK, FL), F32)
    any_ = pl.BlockSpec(memory_space=pl.ANY)
    vm = pl.BlockSpec(memory_space=pltpu.VMEM)
    dma = pltpu.SemaphoreType.DMA
    results = (block, block, block, block, jax.ShapeDtypeStruct((512, 512), BF16))
    return tuple(pl.pallas_call(
        kernel,
        name="fused_step",
        out_shape=tuple(pltpu.VMEM(r.shape, r.dtype) for r in results),
        in_specs=[any_, any_, vm, pl.BlockSpec(memory_space=pltpu.SMEM), vm, any_, any_, any_, any_],
        out_specs=[vm] * 5,
        scratch_shapes=[
            pltpu.VMEM((8 * BLK, FL), BF16),
            pltpu.VMEM((2, 8, BLK, BLK), BF16),
            pltpu.VMEM((2, BLK, 8 * BLK), BF16),
            pltpu.VMEM((2, 8, 64, BLK), BF16),
            pltpu.VMEM((64, 4096), BF16),
            pltpu.VMEM((BLK, FL), BF16),
            pltpu.VMEM((BLK, FL), BF16),
            pltpu.VMEM((8 * BLK, FL), BF16),
            pltpu.VMEM((2, 512, FL), BF16),
            pltpu.VMEM((8, 2, 512, BLK), BF16),
            pltpu.VMEM((2, 4, 512, BLK), BF16),
            pltpu.VMEM((4, 512, BLK), BF16),
            pltpu.VMEM((2, 4, 512, BLK), BF16),
            pltpu.VMEM((8, 2, 512, BLK), BF16),
            dma((16,)),
            dma((45,)), dma((45,)), dma((16,)), dma((16,)), dma((8,)), dma((8,)),
            dma((5,)), dma((5,)), dma((4,)), dma((4,)), dma((28,)), dma((28,)),
            dma((8,)), dma((8,)), dma((4,)), dma((8,)), dma((8,)), dma((16,)),
        ],
        compiler_params=pltpu.CompilerParams(
            collective_id=0, has_side_effects=True, vmem_limit_bytes=52 << 20),
    )(out_grad, hidden_act, log_ratio.reshape(1, 8), pair_order, seq_len.reshape(1, 8),
      master, moment, second, next_act))


def solution(mesh):
    return jax.shard_map(
        body,
        mesh=mesh,
        in_specs=(
            P("dp", None), P("dp", "tensor"), P("dp"), P("dp", None), P("dp"),
            P("dp", "tensor"), P("dp", "tensor"), P("dp", "tensor"), P("dp", "tensor"),
        ),
        out_specs=(P("dp", "tensor"),) * 5,
        check_vma=False,
    )
```

```python
import jax
import jax.numpy as jnp
from jax import lax
from jax.experimental import pallas as pl
from jax.experimental.pallas import tpu as pltpu
from jax.sharding import PartitionSpec as P

LEN = 32
beta_dpo = 0.1
beta_one = 0.9
beta_two = 0.999
bias_one = 1.0 - 0.9**10
bias_two = 1.0 - 0.999**10
adam_eps = 1e-08
rate_learn = 0.001

MESH = pl.DeviceIdType.MESH
F32 = jnp.float32
BF16 = jnp.bfloat16

FL = 1920
BLK = 256
HALF = 128
CHUNKS = ((0, 384), (384, 512), (896, 512), (1408, 384), (1792, 128))
UNIT = 64


def mod4(v):
    return lax.rem(v + 8, 4)


def kernel(
    og_hbm, hid_hbm, ratio_ref, pair_ref, len_ref, mas_hbm, mom_hbm, sec_hbm, nact_hbm,
    MAS, MOM, SEC, ACC, NO,
    H, SC, ST, SS, OG, RSS, RSR, WB, NA, XS, XB, YS, YB, YF,
    loc_sem,
    ha_s, ha_r, sa_s, sa_r, sb_s, sb_r, rs_s, rs_r, na_s, na_r, w_s, w_r, x_s, x_r, y_s, y_r, f_s, f_r,
):
    dp = lax.axis_index("dp")
    tn = lax.axis_index("tensor")
    xl = dp // 8
    z = lax.rem(dp // 2, 4)
    c = lax.rem(dp, 2)
    y = tn // 2
    xh = lax.rem(tn, 2)

    def dev(xl_=None, z_=None, c_=None, y_=None, xh_=None):
        xl_ = xl if xl_ is None else xl_
        z_ = z if z_ is None else z_
        c_ = c if c_ is None else c_
        y_ = y if y_ is None else y_
        xh_ = xh if xh_ is None else xh_
        return (xl_ * 8 + z_ * 2 + c_, y_ * 2 + xh_)

    right, left, far = mod4(z + 1), mod4(z - 1), mod4(z + 2)
    pc = 1 - c

    barrier = pltpu.get_barrier_semaphore()
    for k in range(1, 16):
        idx = lax.rem(xl * 8 + tn + k, 16)
        pl.semaphore_signal(
            barrier, inc=1,
            device_id=((idx // 8) * 8 + z * 2 + c, lax.rem(idx, 8)), device_id_type=MESH)
    for k in range(1, 8):
        idx = lax.rem(z * 2 + c + k, 8)
        pl.semaphore_signal(
            barrier, inc=1, device_id=(xl * 8 + idx, tn), device_id_type=MESH)

    locals_ = []

    def local(src, dst):
        cp = pltpu.make_async_copy(src, dst, loc_sem.at[len(locals_)])
        cp.start()
        locals_.append(cp)
        return cp

    def aligned(v, m):
        return pl.multiple_of(v * m, m)

    qrows = pl.ds(aligned(y, 64), 64)
    og_cp = local(og_hbm.at[qrows, :], OG)
    own_h = local(hid_hbm, H.at[pl.ds(aligned(z * 2 + c, BLK), BLK), :])
    mas_cp = local(mas_hbm, MAS)
    mom_cp = local(mom_hbm, MOM)
    sec_cp = local(sec_hbm, SEC)
    own_na = local(nact_hbm, NA.at[xl])
    sends = []

    def remote(src, dst, ss, rs, to):
        return pltpu.make_async_remote_copy(
            src, dst, ss, rs, device_id=to, device_id_type=MESH)

    def send(src, dst, ss, rs, to):
        cp = remote(src, dst, ss, rs, to)
        cp.start()
        sends.append((None, cp))

    def arrived(dst, ss, rs):
        remote(dst, dst, ss, rs, (dp, tn)).wait_recv()

    def hrow(zz, cc, half=None):
        if half is None:
            return pl.ds(aligned(zz * 2 + cc, BLK), BLK)
        return pl.ds(pl.multiple_of((zz * 2 + cc) * BLK + half * HALF, HALF), HALF)

    def h_own(i):
        cs = pl.ds(CHUNKS[i][0], CHUNKS[i][1])
        src = hid_hbm.at[:, cs]
        dst = H.at[hrow(z, c), cs]
        b = i * 9
        send(src, dst, ha_s.at[b], ha_r.at[b], dev(z_=right))
        send(src, dst, ha_s.at[b + 1], ha_r.at[b + 1], dev(z_=left))
        send(src, dst, ha_s.at[b + 2], ha_r.at[b + 2], dev(c_=pc))

    def h_view(i, zz, cc, half=None):
        return H.at[hrow(zz, cc, half), pl.ds(CHUNKS[i][0], CHUNKS[i][1])]

    def h_forward_near(i):
        b = i * 9
        v = h_view(i, left, c)
        arrived(v, ha_s.at[b], ha_r.at[b])
        v0 = h_view(i, left, c, 0)
        send(v0, v0, ha_s.at[b + 5], ha_r.at[b + 5], dev(z_=right))
        send(v, v, ha_s.at[b + 3], ha_r.at[b + 3], dev(c_=pc))
        v = h_view(i, right, c)
        arrived(v, ha_s.at[b + 1], ha_r.at[b + 1])
        v1 = h_view(i, right, c, 1)
        send(v1, v1, ha_s.at[b + 6], ha_r.at[b + 6], dev(z_=left))
        send(v, v, ha_s.at[b + 4], ha_r.at[b + 4], dev(c_=pc))

    def h_forward_far(i):
        b = i * 9
        for half in (0, 1):
            v = h_view(i, far, c, half)
            arrived(v, ha_s.at[b + 5 + half], ha_r.at[b + 5 + half])
            send(v, v, ha_s.at[b + 7 + half], ha_r.at[b + 7 + half], dev(c_=pc))

    def h_rest(i):
        b = i * 9
        arrived(h_view(i, z, pc), ha_s.at[b + 2], ha_r.at[b + 2])
        arrived(h_view(i, left, pc), ha_s.at[b + 3], ha_r.at[b + 3])
        arrived(h_view(i, right, pc), ha_s.at[b + 4], ha_r.at[b + 4])
        for half in (0, 1):
            arrived(h_view(i, far, pc, half), ha_s.at[b + 7 + half], ha_r.at[b + 7 + half])

    def na_send(p):
        rows = pl.ds(p * HALF, HALF)
        send(nact_hbm.at[rows, :], NA.at[xl, rows, :], na_s.at[p], na_r.at[p], dev(xl_=1 - xl))

    lane = lax.broadcasted_iota(jnp.int32, (1, 8), 1)
    ratios = ratio_ref[...]
    coef = jnp.zeros((1, 8), F32)
    for p in range(4):
        oc = (lane == pair_ref[0, 2 * p]).astype(F32)
        orj = (lane == pair_ref[0, 2 * p + 1]).astype(F32)
        margin = beta_dpo * (
            jnp.sum(oc * ratios, axis=1, keepdims=True)
            - jnp.sum(orj * ratios, axis=1, keepdims=True))
        weight = beta_dpo * jax.nn.sigmoid(-margin)
        coef = coef + weight * (orj - oc)
    row = lax.broadcasted_iota(jnp.int32, (64, 8), 0)
    lane64 = lax.broadcasted_iota(jnp.int32, (64, 8), 1)
    upper = (row >= LEN).astype(jnp.int32)
    sel = (lane64 == 2 * y + upper).astype(F32)
    row_coef = jnp.sum(sel * coef, axis=1, keepdims=True)
    row_len = jnp.sum(sel * len_ref[...].astype(F32), axis=1, keepdims=True)
    pos = (row - LEN * upper)[:, 0:1].astype(F32)
    factor = row_coef * (pos < row_len).astype(F32)
    og_cp.wait()

    def scale(b):
        xlb = (1 - xl) if b == 0 else xl
        for dz in range(4):
            for dc in range(2):
                zz = mod4(z + dz)
                cc = c if dc == 0 else pc
                k = dz * 2 + dc
                cols = pl.ds(aligned(xlb * 8 + zz * 2 + cc, BLK), BLK)
                rows = (OG[:, cols].astype(F32) * factor).astype(BF16)
                if k == 0:
                    SC[b, z * 2 + c, qrows, :] = rows
                else:
                    SS[b, k] = rows

    def scale_send(b):
        for dz in range(4):
            for dc in range(2):
                zz = mod4(z + dz)
                cc = c if dc == 0 else pc
                k = dz * 2 + dc
                if k:
                    send(SS.at[b, k], SC.at[b, z * 2 + c, qrows, :],
                         sa_s.at[b * 8 + k], sa_r.at[b * 8 + k], dev(z_=zz, c_=cc))

    def share_rows(b):
        for dz in range(4):
            for dc in range(2):
                k = dz * 2 + dc
                if k:
                    zz = mod4(z - dz)
                    cc = c if dc == 0 else pc
                    arrived(SC.at[b, zz * 2 + cc, qrows, :], sa_s.at[b * 8 + k], sa_r.at[b * 8 + k])
        for dy in (1, 3, 2):
            v = SC.at[b, :, qrows, :]
            send(v, v, sb_s.at[b * 4 + dy], sb_r.at[b * 4 + dy], dev(y_=mod4(y + dy)))

    def turn(b):
        for dy in (1, 3, 2):
            yy = mod4(y - dy)
            arrived(SC.at[b, :, pl.ds(aligned(yy, 64), 64), :],
                    sb_s.at[b * 4 + dy], sb_r.at[b * 4 + dy])

        @pl.loop(0, 8)
        def _(k):
            ST[b, :, pl.ds(aligned(k, BLK), BLK)] = SC[b, k].T

    def dot_chunk(i, b):
        cs = pl.ds(CHUNKS[i][0], CHUNKS[i][1])
        out = jnp.dot(ST[b], H[:, cs], preferred_element_type=F32)
        if b == 0:
            RSS[:, cs] = out.astype(BF16)
            send(RSS.at[:, cs], RSR.at[:, cs], rs_s.at[i], rs_r.at[i], dev(xl_=1 - xl))
        else:
            ACC[:, cs] = out

    def adam_chunk(i):
        lo, width = CHUNKS[i]
        cs = pl.ds(lo, width)
        arrived(RSR.at[:, cs], rs_s.at[i], rs_r.at[i])
        for s in (0, 1):
            wbase = ((z * 2 + s) * 2 + c) * HALF

            @pl.loop(0, HALF // 16)
            def _(r):
                rows = pl.ds(pl.multiple_of(s * HALF + r * 16, 16), 16)
                wrows = pl.ds(pl.multiple_of(wbase + r * 16, 16), 16)
                grad = ACC[rows, cs] + RSR[rows, cs].astype(F32)
                new_moment = beta_one * MOM[rows, cs] + (1.0 - beta_one) * grad
                new_second = beta_two * SEC[rows, cs] + (1.0 - beta_two) * grad * grad
                update = new_moment / bias_one / (jnp.sqrt(new_second / bias_two) + adam_eps)
                new_master = MAS[rows, cs] - rate_learn * update
                MOM[rows, cs] = new_moment
                SEC[rows, cs] = new_second
                ACC[rows, cs] = update
                MAS[rows, cs] = new_master
                WB[wrows, cs] = new_master.astype(BF16)

    def w_view(zz, u, cc):
        row = ((zz * 2 + u // 2) * 2 + cc) * HALF + (u % 2) * UNIT
        return WB.at[pl.ds(pl.multiple_of(row, UNIT), UNIT), :]

    def w_send(zz, u, n, to):
        v = w_view(zz, u, c)
        send(v, v, w_s.at[u * 9 + n], w_r.at[u * 9 + n], to)

    def w_wait(zz, u, cc, n):
        arrived(w_view(zz, u, cc), w_s.at[u * 9 + n], w_r.at[u * 9 + n])

    def w_part(zz, u, part):
        cols = pl.ds(0, 1408) if part == 0 else pl.ds(1408, 512)
        row = ((zz * 2 + u // 2) * 2 + c) * HALF + (u % 2) * UNIT
        return WB.at[pl.ds(pl.multiple_of(row, UNIT), UNIT), cols]

    def w_own(part):
        for u in range(4):
            v = w_part(z, u, part)
            for n, to in ((0, right), (1, left)):
                k = u * 9 + n + 7 * part
                send(v, v, w_s.at[k], w_r.at[k], dev(z_=to))

    def w_arrived(zz, u, n):
        for part in (0, 1):
            k = u * 9 + n + 7 * part
            arrived(w_part(zz, u, part), w_s.at[k], w_r.at[k])

    def w_near(u):
        w_arrived(left, u, 0)
        if u % 2 == 0:
            w_send(left, u, 5, dev(z_=right))
        w_send(left, u, 3, dev(c_=pc))
        w_arrived(right, u, 1)
        if u % 2 == 1:
            w_send(right, u, 5, dev(z_=left))
        w_send(right, u, 4, dev(c_=pc))

    def w_near_rest(u):
        w_wait(left, u, pc, 3)
        w_wait(right, u, pc, 4)

    def w_far(u):
        w_wait(far, u, c, 5)
        w_send(far, u, 6, dev(c_=pc))

    scale(0)
    scale(1)
    pl.semaphore_wait(barrier, 22)
    scale_send(0)
    h_own(0)
    na_send(0)
    na_send(1)
    scale_send(1)
    h_own(1)
    share_rows(0)
    h_forward_near(0)
    h_own(2)
    share_rows(1)
    h_forward_near(1)
    h_own(3)
    h_forward_far(0)
    own_h.wait()
    turn(0)
    h_rest(0)
    dot_chunk(0, 0)
    h_forward_near(2)
    h_own(4)
    h_forward_far(1)
    h_rest(1)
    dot_chunk(1, 0)
    h_forward_near(3)
    h_forward_far(2)
    h_rest(2)
    dot_chunk(2, 0)
    turn(1)
    dot_chunk(0, 1)
    h_forward_near(4)
    h_forward_far(3)
    h_rest(3)
    dot_chunk(3, 0)
    mas_cp.wait()
    mom_cp.wait()
    sec_cp.wait()
    adam_chunk(0)
    dot_chunk(1, 1)
    adam_chunk(1)
    dot_chunk(2, 1)
    adam_chunk(2)
    w_own(0)
    h_forward_far(4)
    h_rest(4)
    dot_chunk(4, 0)
    na_send(2)
    na_send(3)
    dot_chunk(3, 1)
    dot_chunk(4, 1)
    adam_chunk(3)
    adam_chunk(4)

    w_own(1)
    for u in range(4):
        w_send(z, u, 2, dev(c_=pc))
    own_na.wait()

    def na_wait():
        for p in range(4):
            rows = pl.ds(p * HALF, HALF)
            arrived(NA.at[1 - xl, rows, :], na_s.at[p], na_r.at[p])

    conditional = []

    zzs = (z, 3 - z, mod4(5 - z), far)
    role = mod4(y - 2 * xl)

    def multiply(kind, s, side):
        wcols = pl.ds(aligned(zzs[kind] * 2 + s, BLK), BLK)
        e = kind * 2 + s
        blk = xl if side == 0 else 1 - xl

        @pl.loop(0, 2)
        def _(t):
            rows = pl.ds(aligned(t, BLK), BLK)
            out = lax.dot_general(
                NA[blk, rows, :], WB[wcols, :], (((1,), (1,)), ((), ())),
                preferred_element_type=F32)
            XS[e, side, rows, :] = out.astype(BF16)

    def start_if(go, cp):
        @pl.when(go)
        def _():
            cp.start()

        conditional.append((go, cp))

    def y_start(kind, s, side):
        multiply(kind, s, side)
        e = kind * 2 + s
        n = e * 2 + side
        h = zzs[kind] // 2
        src = XS.at[e, side]
        start_if(role == 2 + h, remote(
            src, YF.at[n, 0], f_s.at[n], f_r.at[2 * n], dev(y_=mod4(2 * xl + 3 - h))))
        start_if(role == 1 - h, remote(
            src, YF.at[n, 1], f_s.at[n], f_r.at[2 * n + 1], dev(y_=2 * xl + h)))

    def y_middle(kind, s, side):
        e = kind * 2 + s
        n = e * 2 + side
        h = zzs[kind] // 2
        go = role == 3 - h

        @pl.when(go)
        def _():
            arrived(YF.at[n, 0], f_s.at[n], f_r.at[2 * n])

            @pl.loop(0, 4)
            def _(r):
                rows = pl.ds(aligned(r, HALF), HALF)
                XS[e, side, rows, :] = (
                    XS[e, side, rows, :].astype(F32) + YF[n, 0, rows, :].astype(F32)).astype(BF16)

        start_if(go, remote(
            XS.at[e, side], YF.at[n, 0], f_s.at[n], f_r.at[2 * n], dev(y_=2 * xl + h)))

    def y_end(kind, s, side):
        e = kind * 2 + s
        n = e * 2 + side
        zz = zzs[kind]
        h = zz // 2
        last = role == h
        blk = xl if side == 0 else 1 - xl

        @pl.when(last)
        def _():
            for g in (0, 1):
                arrived(YF.at[n, g], f_s.at[n], f_r.at[2 * n + g])

            @pl.loop(0, 4)
            def _(r):
                rows = pl.ds(aligned(r, HALF), HALF)
                XS[e, side, rows, :] = (
                    (XS[e, side, rows, :].astype(F32) + YF[n, 1, rows, :].astype(F32))
                    + YF[n, 0, rows, :].astype(F32)).astype(BF16)

        cp = remote(XS.at[e, side], YB.at[s, xh], f_s.at[n], y_r.at[s * 4 + xh],
                    dev(xl_=blk, xh_=lax.rem(zz, 2)))
        if side == 0:
            same = lax.rem(zz, 2) == xh
            start_if(jnp.logical_and(last, jnp.logical_not(same)), cp)

            @pl.when(jnp.logical_and(last, same))
            def _():
                YB[s, xh] = XS[e, side]
        else:
            start_if(last, cp)

    def x_start(kind, s, side):
        multiply(kind, s, side)
        e = kind * 2 + s
        zz = zzs[kind]
        mine = xl * 2 + xh
        blk = xl if side == 0 else 1 - xl
        cp = remote(
            XS.at[e, side], XB.at[s, mine], x_s.at[(e - 4) * 2 + side], x_r.at[s * 4 + mine],
            dev(xl_=blk, xh_=lax.rem(zz, 2)))
        if side == 0:
            stay = lax.rem(zz, 2) == xh
            start_if(jnp.logical_not(stay), cp)

            @pl.when(stay)
            def _():
                XB[s, mine] = XS[e, side]
        else:
            cp.start()
            conditional.append((None, cp))

    def pair_sum(kind, s, side):
        zz = zzs[kind]
        for_me = lax.rem(zz, 2) == xh
        h = xl if side == 0 else 1 - xl
        yd = zz // 2 + 2 * h
        k = s * 2 + side

        @pl.when(for_me)
        def _():
            for g in (0, 1):
                src = h * 2 + g
                if side == 0:
                    @pl.when(g != xh)
                    def _():
                        arrived(XB.at[s, src], x_s.at[0], x_r.at[s * 4 + src])
                else:
                    arrived(XB.at[s, src], x_s.at[0], x_r.at[s * 4 + src])

            @pl.loop(0, 4)
            def _(r):
                rows = pl.ds(aligned(r, HALF), HALF)
                YS[k, rows, :] = (
                    XB[s, h * 2, rows, :].astype(F32)
                    + XB[s, h * 2 + 1, rows, :].astype(F32)).astype(BF16)

        start_if(jnp.logical_and(for_me, yd != y), remote(
            YS.at[k], YB.at[s, y], y_s.at[k], y_r.at[s * 4 + y], dev(y_=yd)))

        @pl.when(jnp.logical_and(for_me, yd == y))
        def _():
            YB[s, y] = YS[k]

    for u in range(4):
        w_wait(z, u, pc, 2)
    y_start(0, 0, 0)
    y_start(0, 1, 0)
    w_near(0)
    w_near(1)
    w_near_rest(0)
    w_near_rest(1)
    y_start(1, 0, 0)
    x_start(2, 0, 0)
    w_near(2)
    w_near(3)
    y_middle(0, 0, 0)
    y_middle(0, 1, 0)
    na_wait()
    x_start(2, 0, 1)
    y_start(0, 0, 1)
    y_start(0, 1, 1)
    y_start(1, 0, 1)
    w_far(0)
    w_far(1)
    w_near_rest(2)
    w_near_rest(3)
    y_middle(1, 0, 0)
    y_end(0, 0, 0)
    y_end(0, 1, 0)
    x_start(2, 1, 0)
    y_start(1, 1, 0)
    w_wait(far, 0, pc, 6)
    w_wait(far, 1, pc, 6)
    x_start(3, 0, 0)
    x_start(3, 0, 1)
    x_start(2, 1, 1)
    y_start(1, 1, 1)
    y_middle(0, 0, 1)
    y_middle(0, 1, 1)
    y_middle(1, 0, 1)
    pair_sum(2, 0, 0)
    pair_sum(2, 0, 1)
    w_far(2)
    w_far(3)
    w_wait(far, 2, pc, 6)
    w_wait(far, 3, pc, 6)
    x_start(3, 1, 0)
    x_start(3, 1, 1)
    pair_sum(3, 0, 0)
    pair_sum(3, 0, 1)
    y_middle(1, 1, 0)
    y_end(1, 0, 0)
    pair_sum(2, 1, 0)
    y_middle(1, 1, 1)
    y_end(0, 0, 1)
    pair_sum(2, 1, 1)
    y_end(0, 1, 1)
    y_end(1, 0, 1)
    pair_sum(3, 1, 0)
    pair_sum(3, 1, 1)
    y_end(1, 1, 0)
    y_end(1, 1, 1)

    zd = lax.rem(y, 2) * 2 + xh
    by_y = jnp.logical_or(zd == z, zd == 3 - z)
    by_x = jnp.logical_not(by_y)

    def finish(s, count):
        @pl.loop(0, 4)
        def _(r):
            rows = pl.ds(aligned(r, HALF), HALF)
            total = YB[s, 0, rows, :].astype(F32) + YB[s, 1, rows, :].astype(F32)
            if count == 4:
                total = total + (YB[s, 2, rows, :].astype(F32) + YB[s, 3, rows, :].astype(F32))
            total = total.astype(BF16)
            NO[rows, s * HALF:(s + 1) * HALF] = total[:, :HALF]
            NO[rows, BLK + s * HALF:BLK + (s + 1) * HALF] = total[:, HALF:]

    for s in (0, 1):
        for g in (0, 1):
            away = jnp.logical_or(y // 2 != xl, g != xh)

            @pl.when(jnp.logical_and(by_y, away))
            def _():
                arrived(YB.at[s, g], y_s.at[0], y_r.at[s * 4 + g])

        for ys in range(4):
            @pl.when(jnp.logical_and(by_x, ys != y))
            def _():
                arrived(YB.at[s, ys], y_s.at[0], y_r.at[s * 4 + ys])

        @pl.when(by_y)
        def _():
            finish(s, 2)

        @pl.when(by_x)
        def _():
            finish(s, 4)

    for go, cp in sends + conditional:
        if go is None:
            cp.wait_send()
        else:
            @pl.when(go)
            def _():
                cp.wait_send()


def body(out_grad, hidden_act, log_ratio, pair_order, seq_len, master, moment, second, next_act):
    block = jax.ShapeDtypeStruct((BLK, FL), F32)
    any_ = pl.BlockSpec(memory_space=pl.ANY)
    vm = pl.BlockSpec(memory_space=pltpu.VMEM)
    dma = pltpu.SemaphoreType.DMA
    results = (block, block, block, block, jax.ShapeDtypeStruct((512, 512), BF16))
    return tuple(pl.pallas_call(
        kernel,
        name="fused_step",
        out_shape=tuple(pltpu.VMEM(r.shape, r.dtype) for r in results),
        in_specs=[any_, any_, vm, pl.BlockSpec(memory_space=pltpu.SMEM), vm, any_, any_, any_, any_],
        out_specs=[vm] * 5,
        scratch_shapes=[
            pltpu.VMEM((8 * BLK, FL), BF16),
            pltpu.VMEM((2, 8, BLK, BLK), BF16),
            pltpu.VMEM((2, BLK, 8 * BLK), BF16),
            pltpu.VMEM((2, 8, 64, BLK), BF16),
            pltpu.VMEM((64, 4096), BF16),
            pltpu.VMEM((BLK, FL), BF16),
            pltpu.VMEM((BLK, FL), BF16),
            pltpu.VMEM((8 * BLK, FL), BF16),
            pltpu.VMEM((2, 512, FL), BF16),
            pltpu.VMEM((8, 2, 512, BLK), BF16),
            pltpu.VMEM((2, 4, 512, BLK), BF16),
            pltpu.VMEM((4, 512, BLK), BF16),
            pltpu.VMEM((2, 4, 512, BLK), BF16),
            pltpu.VMEM((8, 2, 512, BLK), BF16),
            dma((16,)),
            dma((45,)), dma((45,)), dma((16,)), dma((16,)), dma((8,)), dma((8,)),
            dma((5,)), dma((5,)), dma((4,)), dma((4,)), dma((36,)), dma((36,)),
            dma((8,)), dma((8,)), dma((4,)), dma((8,)), dma((8,)), dma((16,)),
        ],
        compiler_params=pltpu.CompilerParams(
            collective_id=0, has_side_effects=True, vmem_limit_bytes=52 << 20),
    )(out_grad, hidden_act, log_ratio.reshape(1, 8), pair_order, seq_len.reshape(1, 8),
      master, moment, second, next_act))


def solution(mesh):
    return jax.shard_map(
        body,
        mesh=mesh,
        in_specs=(
            P("dp", None), P("dp", "tensor"), P("dp"), P("dp", None), P("dp"),
            P("dp", "tensor"), P("dp", "tensor"), P("dp", "tensor"), P("dp", "tensor"),
        ),
        out_specs=(P("dp", "tensor"),) * 5,
        check_vma=False,
    )
```

```python
import jax
import jax.numpy as jnp
from jax import lax
from jax.experimental import pallas as pl
from jax.experimental.pallas import tpu as pltpu
from jax.sharding import PartitionSpec as P

LEN = 32
beta_dpo = 0.1
beta_one = 0.9
beta_two = 0.999
bias_one = 1.0 - 0.9**10
bias_two = 1.0 - 0.999**10
adam_eps = 1e-08
rate_learn = 0.001

MESH = pl.DeviceIdType.MESH
F32 = jnp.float32
BF16 = jnp.bfloat16

FL = 1920
BLK = 256
HALF = 128
CHUNKS = ((0, 256), (256, 512), (768, 640), (1408, 384), (1792, 128))
UNIT = 64


def mod4(v):
    return lax.rem(v + 8, 4)


def kernel(
    og_hbm, hid_hbm, ratio_ref, pair_ref, len_ref, mas_hbm, mom_hbm, sec_hbm, nact_hbm,
    MAS, MOM, SEC, ACC, NO,
    H, SC, ST, SS, OG, RSS, RSR, WB, NA, XS, XB, YS, YB, YF,
    loc_sem,
    ha_s, ha_r, sa_s, sa_r, sb_s, sb_r, rs_s, rs_r, na_s, na_r, w_s, w_r, x_s, x_r, y_s, y_r, f_s, f_r,
):
    dp = lax.axis_index("dp")
    tn = lax.axis_index("tensor")
    xl = dp // 8
    z = lax.rem(dp // 2, 4)
    c = lax.rem(dp, 2)
    y = tn // 2
    xh = lax.rem(tn, 2)

    def dev(xl_=None, z_=None, c_=None, y_=None, xh_=None):
        xl_ = xl if xl_ is None else xl_
        z_ = z if z_ is None else z_
        c_ = c if c_ is None else c_
        y_ = y if y_ is None else y_
        xh_ = xh if xh_ is None else xh_
        return (xl_ * 8 + z_ * 2 + c_, y_ * 2 + xh_)

    right, left, far = mod4(z + 1), mod4(z - 1), mod4(z + 2)
    pc = 1 - c

    barrier = pltpu.get_barrier_semaphore()
    for k in range(1, 16):
        idx = lax.rem(xl * 8 + tn + k, 16)
        pl.semaphore_signal(
            barrier, inc=1,
            device_id=((idx // 8) * 8 + z * 2 + c, lax.rem(idx, 8)), device_id_type=MESH)
    for k in range(1, 8):
        idx = lax.rem(z * 2 + c + k, 8)
        pl.semaphore_signal(
            barrier, inc=1, device_id=(xl * 8 + idx, tn), device_id_type=MESH)

    locals_ = []

    def local(src, dst):
        cp = pltpu.make_async_copy(src, dst, loc_sem.at[len(locals_)])
        cp.start()
        locals_.append(cp)
        return cp

    def aligned(v, m):
        return pl.multiple_of(v * m, m)

    qrows = pl.ds(aligned(y, 64), 64)
    og_cp = local(og_hbm.at[qrows, :], OG)
    own_h = local(hid_hbm, H.at[pl.ds(aligned(z * 2 + c, BLK), BLK), :])
    mas_cp = local(mas_hbm, MAS)
    mom_cp = local(mom_hbm, MOM)
    sec_cp = local(sec_hbm, SEC)
    own_na = local(nact_hbm, NA.at[xl])
    sends = []

    def remote(src, dst, ss, rs, to):
        return pltpu.make_async_remote_copy(
            src, dst, ss, rs, device_id=to, device_id_type=MESH)

    def send(src, dst, ss, rs, to):
        cp = remote(src, dst, ss, rs, to)
        cp.start()
        sends.append((None, cp))

    def arrived(dst, ss, rs):
        remote(dst, dst, ss, rs, (dp, tn)).wait_recv()

    def hrow(zz, cc, half=None):
        if half is None:
            return pl.ds(aligned(zz * 2 + cc, BLK), BLK)
        return pl.ds(pl.multiple_of((zz * 2 + cc) * BLK + half * HALF, HALF), HALF)

    def h_own(i):
        cs = pl.ds(CHUNKS[i][0], CHUNKS[i][1])
        src = hid_hbm.at[:, cs]
        dst = H.at[hrow(z, c), cs]
        b = i * 9
        send(src, dst, ha_s.at[b], ha_r.at[b], dev(z_=right))
        send(src, dst, ha_s.at[b + 1], ha_r.at[b + 1], dev(z_=left))
        send(src, dst, ha_s.at[b + 2], ha_r.at[b + 2], dev(c_=pc))

    def h_view(i, zz, cc, half=None):
        return H.at[hrow(zz, cc, half), pl.ds(CHUNKS[i][0], CHUNKS[i][1])]

    def h_forward_near(i):
        b = i * 9
        v = h_view(i, left, c)
        arrived(v, ha_s.at[b], ha_r.at[b])
        v0 = h_view(i, left, c, 0)
        send(v0, v0, ha_s.at[b + 5], ha_r.at[b + 5], dev(z_=right))
        send(v, v, ha_s.at[b + 3], ha_r.at[b + 3], dev(c_=pc))
        v = h_view(i, right, c)
        arrived(v, ha_s.at[b + 1], ha_r.at[b + 1])
        v1 = h_view(i, right, c, 1)
        send(v1, v1, ha_s.at[b + 6], ha_r.at[b + 6], dev(z_=left))
        send(v, v, ha_s.at[b + 4], ha_r.at[b + 4], dev(c_=pc))

    def h_forward_far(i):
        b = i * 9
        for half in (0, 1):
            v = h_view(i, far, c, half)
            arrived(v, ha_s.at[b + 5 + half], ha_r.at[b + 5 + half])
            send(v, v, ha_s.at[b + 7 + half], ha_r.at[b + 7 + half], dev(c_=pc))

    def h_rest(i):
        b = i * 9
        arrived(h_view(i, z, pc), ha_s.at[b + 2], ha_r.at[b + 2])
        arrived(h_view(i, left, pc), ha_s.at[b + 3], ha_r.at[b + 3])
        arrived(h_view(i, right, pc), ha_s.at[b + 4], ha_r.at[b + 4])
        for half in (0, 1):
            arrived(h_view(i, far, pc, half), ha_s.at[b + 7 + half], ha_r.at[b + 7 + half])

    def na_send(p):
        rows = pl.ds(p * HALF, HALF)
        send(nact_hbm.at[rows, :], NA.at[xl, rows, :], na_s.at[p], na_r.at[p], dev(xl_=1 - xl))

    lane = lax.broadcasted_iota(jnp.int32, (1, 8), 1)
    ratios = ratio_ref[...]
    coef = jnp.zeros((1, 8), F32)
    for p in range(4):
        oc = (lane == pair_ref[0, 2 * p]).astype(F32)
        orj = (lane == pair_ref[0, 2 * p + 1]).astype(F32)
        margin = beta_dpo * (
            jnp.sum(oc * ratios, axis=1, keepdims=True)
            - jnp.sum(orj * ratios, axis=1, keepdims=True))
        weight = beta_dpo * jax.nn.sigmoid(-margin)
        coef = coef + weight * (orj - oc)
    row = lax.broadcasted_iota(jnp.int32, (64, 8), 0)
    lane64 = lax.broadcasted_iota(jnp.int32, (64, 8), 1)
    upper = (row >= LEN).astype(jnp.int32)
    sel = (lane64 == 2 * y + upper).astype(F32)
    row_coef = jnp.sum(sel * coef, axis=1, keepdims=True)
    row_len = jnp.sum(sel * len_ref[...].astype(F32), axis=1, keepdims=True)
    pos = (row - LEN * upper)[:, 0:1].astype(F32)
    factor = row_coef * (pos < row_len).astype(F32)
    og_cp.wait()

    def scale(b):
        xlb = (1 - xl) if b == 0 else xl
        for dz in range(4):
            for dc in range(2):
                zz = mod4(z + dz)
                cc = c if dc == 0 else pc
                k = dz * 2 + dc
                cols = pl.ds(aligned(xlb * 8 + zz * 2 + cc, BLK), BLK)
                rows = (OG[:, cols].astype(F32) * factor).astype(BF16)
                if k == 0:
                    SC[b, z * 2 + c, qrows, :] = rows
                else:
                    SS[b, k] = rows

    def scale_send(b):
        for dz in range(4):
            for dc in range(2):
                zz = mod4(z + dz)
                cc = c if dc == 0 else pc
                k = dz * 2 + dc
                if k:
                    send(SS.at[b, k], SC.at[b, z * 2 + c, qrows, :],
                         sa_s.at[b * 8 + k], sa_r.at[b * 8 + k], dev(z_=zz, c_=cc))

    def share_rows(b):
        for dz in range(4):
            for dc in range(2):
                k = dz * 2 + dc
                if k:
                    zz = mod4(z - dz)
                    cc = c if dc == 0 else pc
                    arrived(SC.at[b, zz * 2 + cc, qrows, :], sa_s.at[b * 8 + k], sa_r.at[b * 8 + k])
        for dy in (1, 3, 2):
            v = SC.at[b, :, qrows, :]
            send(v, v, sb_s.at[b * 4 + dy], sb_r.at[b * 4 + dy], dev(y_=mod4(y + dy)))

    def turn(b):
        for dy in (1, 3, 2):
            yy = mod4(y - dy)
            arrived(SC.at[b, :, pl.ds(aligned(yy, 64), 64), :],
                    sb_s.at[b * 4 + dy], sb_r.at[b * 4 + dy])

        @pl.loop(0, 8)
        def _(k):
            ST[b, :, pl.ds(aligned(k, BLK), BLK)] = SC[b, k].T

    def dot_chunk(i, b):
        cs = pl.ds(CHUNKS[i][0], CHUNKS[i][1])
        out = jnp.dot(ST[b], H[:, cs], preferred_element_type=F32)
        if b == 0:
            RSS[:, cs] = out.astype(BF16)
            send(RSS.at[:, cs], RSR.at[:, cs], rs_s.at[i], rs_r.at[i], dev(xl_=1 - xl))
        else:
            ACC[:, cs] = out

    def adam_chunk(i):
        lo, width = CHUNKS[i]
        cs = pl.ds(lo, width)
        arrived(RSR.at[:, cs], rs_s.at[i], rs_r.at[i])
        for s in (0, 1):
            wbase = ((z * 2 + s) * 2 + c) * HALF

            @pl.loop(0, HALF // 16)
            def _(r):
                rows = pl.ds(pl.multiple_of(s * HALF + r * 16, 16), 16)
                wrows = pl.ds(pl.multiple_of(wbase + r * 16, 16), 16)
                grad = ACC[rows, cs] + RSR[rows, cs].astype(F32)
                new_moment = beta_one * MOM[rows, cs] + (1.0 - beta_one) * grad
                new_second = beta_two * SEC[rows, cs] + (1.0 - beta_two) * grad * grad
                update = new_moment / bias_one / (jnp.sqrt(new_second / bias_two) + adam_eps)
                new_master = MAS[rows, cs] - rate_learn * update
                MOM[rows, cs] = new_moment
                SEC[rows, cs] = new_second
                ACC[rows, cs] = update
                MAS[rows, cs] = new_master
                WB[wrows, cs] = new_master.astype(BF16)

    def w_view(zz, u, cc):
        row = ((zz * 2 + u // 2) * 2 + cc) * HALF + (u % 2) * UNIT
        return WB.at[pl.ds(pl.multiple_of(row, UNIT), UNIT), :]

    def w_send(zz, u, n, to):
        v = w_view(zz, u, c)
        send(v, v, w_s.at[u * 9 + n], w_r.at[u * 9 + n], to)

    def w_wait(zz, u, cc, n):
        arrived(w_view(zz, u, cc), w_s.at[u * 9 + n], w_r.at[u * 9 + n])

    def w_part(zz, u, part):
        cols = pl.ds(0, 1408) if part == 0 else pl.ds(1408, 512)
        row = ((zz * 2 + u // 2) * 2 + c) * HALF + (u % 2) * UNIT
        return WB.at[pl.ds(pl.multiple_of(row, UNIT), UNIT), cols]

    def w_own(part):
        for u in range(4):
            v = w_part(z, u, part)
            for n, to in ((0, right), (1, left)):
                k = u * 9 + n + 7 * part
                send(v, v, w_s.at[k], w_r.at[k], dev(z_=to))

    def w_arrived(zz, u, n):
        for part in (0, 1):
            k = u * 9 + n + 7 * part
            arrived(w_part(zz, u, part), w_s.at[k], w_r.at[k])

    def w_near(u):
        w_arrived(left, u, 0)
        if u % 2 == 0:
            w_send(left, u, 5, dev(z_=right))
        w_send(left, u, 3, dev(c_=pc))
        w_arrived(right, u, 1)
        if u % 2 == 1:
            w_send(right, u, 5, dev(z_=left))
        w_send(right, u, 4, dev(c_=pc))

    def w_near_rest(u):
        w_wait(left, u, pc, 3)
        w_wait(right, u, pc, 4)

    def w_far(u):
        w_wait(far, u, c, 5)
        w_send(far, u, 6, dev(c_=pc))

    scale(0)
    scale(1)
    pl.semaphore_wait(barrier, 22)
    scale_send(0)
    h_own(0)
    na_send(0)
    na_send(1)
    scale_send(1)
    h_own(1)
    share_rows(0)
    h_forward_near(0)
    h_own(2)
    share_rows(1)
    h_forward_near(1)
    h_own(3)
    h_forward_far(0)
    own_h.wait()
    turn(0)
    h_rest(0)
    dot_chunk(0, 0)
    h_forward_near(2)
    h_own(4)
    h_forward_far(1)
    h_rest(1)
    dot_chunk(1, 0)
    h_forward_near(3)
    h_forward_far(2)
    h_rest(2)
    dot_chunk(2, 0)
    turn(1)
    dot_chunk(0, 1)
    h_forward_near(4)
    h_forward_far(3)
    h_rest(3)
    dot_chunk(3, 0)
    mas_cp.wait()
    mom_cp.wait()
    sec_cp.wait()
    adam_chunk(0)
    dot_chunk(1, 1)
    adam_chunk(1)
    dot_chunk(2, 1)
    adam_chunk(2)
    w_own(0)
    h_forward_far(4)
    h_rest(4)
    dot_chunk(4, 0)
    na_send(2)
    na_send(3)
    dot_chunk(3, 1)
    dot_chunk(4, 1)
    adam_chunk(3)
    adam_chunk(4)

    w_own(1)
    for u in range(4):
        w_send(z, u, 2, dev(c_=pc))
    own_na.wait()

    def na_wait():
        for p in range(4):
            rows = pl.ds(p * HALF, HALF)
            arrived(NA.at[1 - xl, rows, :], na_s.at[p], na_r.at[p])

    conditional = []

    zzs = (z, 3 - z, mod4(5 - z), far)
    role = mod4(y - 2 * xl)

    def multiply(kind, s, side):
        wcols = pl.ds(aligned(zzs[kind] * 2 + s, BLK), BLK)
        e = kind * 2 + s
        blk = xl if side == 0 else 1 - xl

        @pl.loop(0, 2)
        def _(t):
            rows = pl.ds(aligned(t, BLK), BLK)
            out = lax.dot_general(
                NA[blk, rows, :], WB[wcols, :], (((1,), (1,)), ((), ())),
                preferred_element_type=F32)
            XS[e, side, rows, :] = out.astype(BF16)

    def start_if(go, cp):
        @pl.when(go)
        def _():
            cp.start()

        conditional.append((go, cp))

    def y_start(kind, s, side):
        multiply(kind, s, side)
        e = kind * 2 + s
        n = e * 2 + side
        h = zzs[kind] // 2
        src = XS.at[e, side]
        start_if(role == 2 + h, remote(
            src, YF.at[n, 0], f_s.at[n], f_r.at[2 * n], dev(y_=mod4(2 * xl + 3 - h))))
        start_if(role == 1 - h, remote(
            src, YF.at[n, 1], f_s.at[n], f_r.at[2 * n + 1], dev(y_=2 * xl + h)))

    def y_middle(kind, s, side):
        e = kind * 2 + s
        n = e * 2 + side
        h = zzs[kind] // 2
        go = role == 3 - h

        @pl.when(go)
        def _():
            arrived(YF.at[n, 0], f_s.at[n], f_r.at[2 * n])

            @pl.loop(0, 4)
            def _(r):
                rows = pl.ds(aligned(r, HALF), HALF)
                XS[e, side, rows, :] = (
                    XS[e, side, rows, :].astype(F32) + YF[n, 0, rows, :].astype(F32)).astype(BF16)

        start_if(go, remote(
            XS.at[e, side], YF.at[n, 0], f_s.at[n], f_r.at[2 * n], dev(y_=2 * xl + h)))

    def y_end(kind, s, side):
        e = kind * 2 + s
        n = e * 2 + side
        zz = zzs[kind]
        h = zz // 2
        last = role == h
        blk = xl if side == 0 else 1 - xl

        @pl.when(last)
        def _():
            for g in (0, 1):
                arrived(YF.at[n, g], f_s.at[n], f_r.at[2 * n + g])

            @pl.loop(0, 4)
            def _(r):
                rows = pl.ds(aligned(r, HALF), HALF)
                XS[e, side, rows, :] = (
                    (XS[e, side, rows, :].astype(F32) + YF[n, 1, rows, :].astype(F32))
                    + YF[n, 0, rows, :].astype(F32)).astype(BF16)

        cp = remote(XS.at[e, side], YB.at[s, xh], f_s.at[n], y_r.at[s * 4 + xh],
                    dev(xl_=blk, xh_=lax.rem(zz, 2)))
        if side == 0:
            same = lax.rem(zz, 2) == xh
            start_if(jnp.logical_and(last, jnp.logical_not(same)), cp)

            @pl.when(jnp.logical_and(last, same))
            def _():
                YB[s, xh] = XS[e, side]
        else:
            start_if(last, cp)

    def x_start(kind, s, side):
        multiply(kind, s, side)
        e = kind * 2 + s
        zz = zzs[kind]
        mine = xl * 2 + xh
        blk = xl if side == 0 else 1 - xl
        cp = remote(
            XS.at[e, side], XB.at[s, mine], x_s.at[(e - 4) * 2 + side], x_r.at[s * 4 + mine],
            dev(xl_=blk, xh_=lax.rem(zz, 2)))
        if side == 0:
            stay = lax.rem(zz, 2) == xh
            start_if(jnp.logical_not(stay), cp)

            @pl.when(stay)
            def _():
                XB[s, mine] = XS[e, side]
        else:
            cp.start()
            conditional.append((None, cp))

    def pair_sum(kind, s, side):
        zz = zzs[kind]
        for_me = lax.rem(zz, 2) == xh
        h = xl if side == 0 else 1 - xl
        yd = zz // 2 + 2 * h
        k = s * 2 + side

        @pl.when(for_me)
        def _():
            for g in (0, 1):
                src = h * 2 + g
                if side == 0:
                    @pl.when(g != xh)
                    def _():
                        arrived(XB.at[s, src], x_s.at[0], x_r.at[s * 4 + src])
                else:
                    arrived(XB.at[s, src], x_s.at[0], x_r.at[s * 4 + src])

            @pl.loop(0, 4)
            def _(r):
                rows = pl.ds(aligned(r, HALF), HALF)
                YS[k, rows, :] = (
                    XB[s, h * 2, rows, :].astype(F32)
                    + XB[s, h * 2 + 1, rows, :].astype(F32)).astype(BF16)

        start_if(jnp.logical_and(for_me, yd != y), remote(
            YS.at[k], YB.at[s, y], y_s.at[k], y_r.at[s * 4 + y], dev(y_=yd)))

        @pl.when(jnp.logical_and(for_me, yd == y))
        def _():
            YB[s, y] = YS[k]

    for u in range(4):
        w_wait(z, u, pc, 2)
    y_start(0, 0, 0)
    y_start(0, 1, 0)
    w_near(0)
    w_near(1)
    w_near_rest(0)
    w_near_rest(1)
    y_start(1, 0, 0)
    x_start(2, 0, 0)
    w_near(2)
    w_near(3)
    y_middle(0, 0, 0)
    y_middle(0, 1, 0)
    na_wait()
    x_start(2, 0, 1)
    y_start(0, 0, 1)
    y_start(0, 1, 1)
    y_start(1, 0, 1)
    w_far(0)
    w_far(1)
    w_near_rest(2)
    w_near_rest(3)
    y_middle(1, 0, 0)
    y_end(0, 0, 0)
    y_end(0, 1, 0)
    x_start(2, 1, 0)
    y_start(1, 1, 0)
    w_wait(far, 0, pc, 6)
    w_wait(far, 1, pc, 6)
    x_start(3, 0, 0)
    x_start(3, 0, 1)
    x_start(2, 1, 1)
    y_start(1, 1, 1)
    y_middle(0, 0, 1)
    y_middle(0, 1, 1)
    y_middle(1, 0, 1)
    pair_sum(2, 0, 0)
    pair_sum(2, 0, 1)
    w_far(2)
    w_far(3)
    w_wait(far, 2, pc, 6)
    w_wait(far, 3, pc, 6)
    x_start(3, 1, 0)
    x_start(3, 1, 1)
    pair_sum(3, 0, 0)
    pair_sum(3, 0, 1)
    y_middle(1, 1, 0)
    y_end(1, 0, 0)
    pair_sum(2, 1, 0)
    y_middle(1, 1, 1)
    y_end(0, 0, 1)
    pair_sum(2, 1, 1)
    y_end(0, 1, 1)
    y_end(1, 0, 1)
    pair_sum(3, 1, 0)
    pair_sum(3, 1, 1)
    y_end(1, 1, 0)
    y_end(1, 1, 1)

    zd = lax.rem(y, 2) * 2 + xh
    by_y = jnp.logical_or(zd == z, zd == 3 - z)
    by_x = jnp.logical_not(by_y)

    def finish(s, count):
        @pl.loop(0, 4)
        def _(r):
            rows = pl.ds(aligned(r, HALF), HALF)
            total = YB[s, 0, rows, :].astype(F32) + YB[s, 1, rows, :].astype(F32)
            if count == 4:
                total = total + (YB[s, 2, rows, :].astype(F32) + YB[s, 3, rows, :].astype(F32))
            total = total.astype(BF16)
            NO[rows, s * HALF:(s + 1) * HALF] = total[:, :HALF]
            NO[rows, BLK + s * HALF:BLK + (s + 1) * HALF] = total[:, HALF:]

    for s in (0, 1):
        for g in (0, 1):
            away = jnp.logical_or(y // 2 != xl, g != xh)

            @pl.when(jnp.logical_and(by_y, away))
            def _():
                arrived(YB.at[s, g], y_s.at[0], y_r.at[s * 4 + g])

        for ys in range(4):
            @pl.when(jnp.logical_and(by_x, ys != y))
            def _():
                arrived(YB.at[s, ys], y_s.at[0], y_r.at[s * 4 + ys])

        @pl.when(by_y)
        def _():
            finish(s, 2)

        @pl.when(by_x)
        def _():
            finish(s, 4)

    for go, cp in sends + conditional:
        if go is None:
            cp.wait_send()
        else:
            @pl.when(go)
            def _():
                cp.wait_send()


def body(out_grad, hidden_act, log_ratio, pair_order, seq_len, master, moment, second, next_act):
    block = jax.ShapeDtypeStruct((BLK, FL), F32)
    any_ = pl.BlockSpec(memory_space=pl.ANY)
    vm = pl.BlockSpec(memory_space=pltpu.VMEM)
    dma = pltpu.SemaphoreType.DMA
    results = (block, block, block, block, jax.ShapeDtypeStruct((512, 512), BF16))
    return tuple(pl.pallas_call(
        kernel,
        name="fused_step",
        out_shape=tuple(pltpu.VMEM(r.shape, r.dtype) for r in results),
        in_specs=[any_, any_, vm, pl.BlockSpec(memory_space=pltpu.SMEM), vm, any_, any_, any_, any_],
        out_specs=[vm] * 5,
        scratch_shapes=[
            pltpu.VMEM((8 * BLK, FL), BF16),
            pltpu.VMEM((2, 8, BLK, BLK), BF16),
            pltpu.VMEM((2, BLK, 8 * BLK), BF16),
            pltpu.VMEM((2, 8, 64, BLK), BF16),
            pltpu.VMEM((64, 4096), BF16),
            pltpu.VMEM((BLK, FL), BF16),
            pltpu.VMEM((BLK, FL), BF16),
            pltpu.VMEM((8 * BLK, FL), BF16),
            pltpu.VMEM((2, 512, FL), BF16),
            pltpu.VMEM((8, 2, 512, BLK), BF16),
            pltpu.VMEM((2, 4, 512, BLK), BF16),
            pltpu.VMEM((4, 512, BLK), BF16),
            pltpu.VMEM((2, 4, 512, BLK), BF16),
            pltpu.VMEM((8, 2, 512, BLK), BF16),
            dma((16,)),
            dma((45,)), dma((45,)), dma((16,)), dma((16,)), dma((8,)), dma((8,)),
            dma((5,)), dma((5,)), dma((4,)), dma((4,)), dma((36,)), dma((36,)),
            dma((8,)), dma((8,)), dma((4,)), dma((8,)), dma((8,)), dma((16,)),
        ],
        compiler_params=pltpu.CompilerParams(
            collective_id=0, has_side_effects=True, vmem_limit_bytes=52 << 20),
    )(out_grad, hidden_act, log_ratio.reshape(1, 8), pair_order, seq_len.reshape(1, 8),
      master, moment, second, next_act))


def solution(mesh):
    return jax.shard_map(
        body,
        mesh=mesh,
        in_specs=(
            P("dp", None), P("dp", "tensor"), P("dp"), P("dp", None), P("dp"),
            P("dp", "tensor"), P("dp", "tensor"), P("dp", "tensor"), P("dp", "tensor"),
        ),
        out_specs=(P("dp", "tensor"),) * 5,
        check_vma=False,
    )
```
